512 devices in a mesh: seq: 64 (over y, z), head: 8 (over x, core).
Axes of the slice: x: 4, y: 4, z: 16, core: 2. Of those that a mesh axis runs over, the one named last changes fastest.
Arguments:
- hidden_in: bfloat16 [16384, 4096], P('seq', 'head'), may hold values from -6 to 6
- proj_weight: bfloat16 [4096, 256], replicated, may hold values from -0.09375 to 0.09375
- head_input: bfloat16 [16384, 8192], P('seq', 'head'), may hold values from -6 to 6
- gate_input: bfloat16 [16384, 8192], P('seq', 'head'), may hold values from -11 to 11
- step_size: float32 [16384, 128], P('seq', 'head'), may hold values from 0 to 4, as said below
- decay_rate: float32 [128], P('head'), may hold values from 0 to 1, as said below
- norm_gain: float32 [8192], P('head'), may hold values from 0.1 to 1.9
Outputs:
- layer_out: bfloat16 [16384, 8192], P('seq', 'head')
The draws below stay inside these ranges and needn't reach their ends.
Inputs may be any that keep to these rules, and one draw needn't show every extreme that they name: `decay_rate`: positive. `step_size`: positive.
All inputs are finite; a program needn't handle non-finite values.
Results may differ from the reference program's by a relative error of at most 0.013.
Values may be sent and summed in bfloat16 or wider, within the bound.
A program may use at most 128 MiB of HBM per device.

```python
import math
import jax
import jax.numpy as jnp
from jax import lax

D = 4096
HEADS = 128
HEAD_DIM = 64
STATE = 128
GROUP = 256
TOK_DEV = 256
TOKENS = 16384


def slow_heads(key):
    picked = jax.random.uniform(jax.random.fold_in(key, 101), (HEADS,))
    share = 0.5
    return picked < share


def slow_scale():
    return math.sqrt(32.0 / TOKENS)


def draw_step_size(key, part):
    slow = slow_heads(key)
    head_scale = jnp.where(slow, slow_scale(), 1.0)
    blocks = TOKENS // TOK_DEV
    spread = jnp.where(slow, math.log(4.0), math.log(2.0))
    level = jax.random.uniform(jax.random.fold_in(key, 202), (blocks, HEADS), minval=-1.0, maxval=1.0)
    factor = jnp.exp(level * spread[None, :])
    factor = jnp.repeat(factor, TOK_DEV, axis=0)
    jitter = jax.random.uniform(jax.random.fold_in(key, 303), (TOKENS, HEADS), minval=0.6, maxval=1.4)
    return (head_scale[None, :] * factor * jitter).astype(jnp.float32)


def draw_decay_rate(key, part):
    slow = slow_heads(key)
    slow_rate = jnp.exp(jax.random.uniform(jax.random.fold_in(key, 404), (HEADS,), minval=math.log(0.3), maxval=math.log(1.2))) / (TOKENS * slow_scale())
    fast_rate = jnp.exp(jax.random.uniform(jax.random.fold_in(key, 505), (HEADS,), minval=math.log(1.0 / 250.0), maxval=math.log(1.0 / 30.0)))
    return jnp.where(slow, slow_rate, fast_rate).astype(jnp.float32)


def draw_gate_input(key, part):
    columns = HEADS * HEAD_DIM
    ramp = jnp.arange(columns, dtype=jnp.float32) / (columns - 1)
    values = jnp.clip(jax.random.normal(jax.random.fold_in(key, 606), (TOKENS, columns), jnp.float32), -5.0, 5.0)
    values = values * (0.6 + 1.2 * ramp)[None, :]
    return values.astype(jnp.bfloat16)


def block_levels(rng, dims, cuts, least, high):
    def one(axis_at, shards_of):
        heights = jax.random.uniform(jax.random.fold_in(jax.random.fold_in(rng, 6), axis_at), (shards_of,), jnp.float32, least / len(cuts), high / len(cuts))
        return jnp.repeat(jnp.exp(heights), dims[axis_at] // shards_of).reshape((-1,) + (1,) * (len(dims) - axis_at - 1))

    factor_of = one(*cuts[0])
    for cut in cuts[1:]:
        factor_of = factor_of * one(*cut)
    return factor_of


def bell_draw(own_key, extent, scale, bound, shards=(), kind=jnp.bfloat16):
    values = jax.random.normal(own_key, extent, jnp.float32) * scale
    if len(shards) > 0:
        values = block_levels(own_key, extent, shards, -0.22, 0.18) * values
    return jnp.clip(values, min=-bound, max=bound).astype(kind)


def setup_inputs(seed: int = 0) -> dict:
    key_list = jax.random.split(jax.random.key(seed), 8)
    return {
        "hidden_in": bell_draw(key_list[0], (TOKENS, D), 1.0, 6.0, ((0, 64), (1, 8))),
        "proj_weight": bell_draw(key_list[1], (D, 2 * STATE), D ** -0.5, 0.09375),
        "head_input": bell_draw(key_list[2], (TOKENS, HEADS * HEAD_DIM), 1.0, 6.0, ((0, 64), (1, 8))),
        "gate_input": draw_gate_input(jax.random.fold_in(key_list[7], 71), 0),
        "step_size": draw_step_size(jax.random.fold_in(key_list[7], 71), 0),
        "decay_rate": draw_decay_rate(jax.random.fold_in(key_list[7], 71), 0),
        "norm_gain": jnp.clip(1.0 + 0.18 * jax.random.normal(key_list[6], (HEADS * HEAD_DIM,), jnp.float32), 0.1, 1.9),
    }


def reference(hidden_in, proj_weight, head_input, gate_input, step_size, decay_rate, norm_gain):
    projected = jnp.dot(hidden_in, proj_weight, preferred_element_type=jnp.float32).astype(jnp.bfloat16)
    count = TOKENS // GROUP
    b_rows = projected[:, :STATE].reshape(count, GROUP, STATE)
    c_rows = projected[:, STATE:].reshape(count, GROUP, STATE)
    log_decay = -step_size * decay_rate[None, :]
    cumulative = jnp.cumsum(log_decay.reshape(count, GROUP, HEADS), axis=1)
    scaled = (head_input.reshape(TOKENS, HEADS, HEAD_DIM).astype(jnp.float32) * step_size[:, :, None]).astype(jnp.bfloat16)
    scaled = scaled.reshape(count, GROUP, HEADS, HEAD_DIM)
    positions = jnp.arange(GROUP, dtype=jnp.int32)
    causal = positions[:, None] >= positions[None, :]

    def one_group(carried, pieces):
        b_here, c_here, cum_here, x_here = pieces
        scores = jnp.dot(c_here, b_here.T, preferred_element_type=jnp.float32)
        cum_heads = cum_here.T
        gap = cum_heads[:, :, None] - cum_heads[:, None, :]
        weights = jnp.exp(jnp.where(causal[None], gap, -jnp.inf))
        mixing = lax.optimization_barrier((scores[None] * weights).astype(jnp.bfloat16))
        inner = jnp.einsum('hts,shp->thp', mixing.astype(jnp.float32), x_here.astype(jnp.float32))
        carried_low = lax.optimization_barrier(carried.astype(jnp.bfloat16))
        outer = jnp.einsum('tn,hpn->thp', c_here.astype(jnp.float32), carried_low.astype(jnp.float32))
        outer = outer * jnp.exp(cum_here)[:, :, None]
        tail = jnp.exp(cum_here[-1][None, :] - cum_here)
        weighted = lax.optimization_barrier((tail[:, :, None] * x_here.astype(jnp.float32)).astype(jnp.bfloat16))
        fresh = jnp.einsum('shp,sn->hpn', weighted.astype(jnp.float32), b_here.astype(jnp.float32))
        updated = jnp.exp(cum_here[-1])[:, None, None] * carried + fresh
        return (updated, inner + outer)
    start = jnp.zeros((HEADS, HEAD_DIM, STATE), jnp.float32)
    final, outputs = lax.scan(one_group, start, (b_rows, c_rows, cumulative, scaled))
    mixed = outputs.reshape(TOKENS, HEADS * HEAD_DIM)
    gated = mixed * jax.nn.silu(gate_input.astype(jnp.float32))
    mean_square = lax.optimization_barrier(jnp.mean(gated * gated, axis=1, keepdims=True))
    return (gated * lax.rsqrt(mean_square + 1e-05) * norm_gain[None, :]).astype(jnp.bfloat16)
```

```python
import functools
import math

import jax
import jax.numpy as jnp
from jax import lax
from jax.experimental import pallas as pl
from jax.experimental.pallas import tpu as pltpu
from jax.sharding import PartitionSpec as P

MESH = pl.DeviceIdType.MESH
F32, BF16 = jnp.float32, jnp.bfloat16
T = 256
HEADS = 16
HEAD_DIM = 64
STATE = 128
COLS = HEADS * HEAD_DIM
HALF = COLS // 2
LOG2E = math.log2(math.e)


def dot(a, b):
    return jnp.dot(a, b, preferred_element_type=F32)


def kernel(
    NH, NY, NZ,
    hid, w, x, g, dt, rate, gain, out,
    hid_v, w_v, x_v, g_v, dt_v, rate_v, gain_v, in_sem,
    part, rsr, agr, scl, wgt, expand,
    fsend, frecv, dsend, drecv, ysend, yrecv, gsend, grecv,
    acc, fac, gated_v, srecv,
    rs_s, rs_r, ag_s, ag_r, d_s, d_r, f_s, f_r, y_s, y_r, g_s, g_r, s_s, s_r,
):
    KD = hid_v.shape[1]
    RB = T // NH
    NI = NZ // 2
    me_h = lax.axis_index("head")
    seq = lax.axis_index("seq")
    me_z = lax.rem(seq, NZ)
    me_y = lax.div(seq, NZ)

    def head_peer(r):
        return lax.rem(me_h + r, NH)

    def z_peer(r):
        return lax.rem(me_z + r, NZ)

    def y_peer(r):
        return lax.rem(me_y + r, NY)

    def seq_id(y, z):
        return y * NZ + z

    barrier = pltpu.get_barrier_semaphore()

    @pl.loop(1, NH)
    def _(r):
        pl.semaphore_signal(barrier, inc=1, device_id={"head": head_peer(r)}, device_id_type=MESH)

    @pl.loop(1, NZ)
    def _(r):
        pl.semaphore_signal(barrier, inc=1, device_id={"seq": seq_id(me_y, z_peer(r))}, device_id_type=MESH)

    @pl.loop(1, NY)
    def _(r):
        pl.semaphore_signal(barrier, inc=1, device_id={"seq": seq_id(y_peer(r), me_z)}, device_id_type=MESH)

    loads = [
        pltpu.make_async_copy(hid, hid_v, in_sem.at[0]),
        pltpu.make_async_copy(w.at[pl.ds(pl.multiple_of(me_h * KD, KD), KD)], w_v, in_sem.at[1]),
        pltpu.make_async_copy(dt, dt_v, in_sem.at[2]),
        pltpu.make_async_copy(rate, rate_v, in_sem.at[3]),
        pltpu.make_async_copy(x, x_v, in_sem.at[4]),
        pltpu.make_async_copy(g, g_v, in_sem.at[5]),
        pltpu.make_async_copy(gain, gain_v, in_sem.at[6]),
    ]
    for load in loads:
        load.start()
    loads[0].wait()
    loads[1].wait()
    part[...] = dot(hid_v[...], w_v[...]).reshape(NH, RB, 2 * STATE)

    def rs_copy(src, dst_peer, slot):
        return pltpu.make_async_remote_copy(
            src_ref=part.at[src], dst_ref=rsr.at[slot], send_sem=rs_s.at[src], recv_sem=rs_r.at[slot],
            device_id={"head": dst_peer}, device_id_type=MESH)

    def ag_copy(peer, slot):
        return pltpu.make_async_remote_copy(
            src_ref=agr.at[slot], dst_ref=agr.at[slot], send_sem=ag_s.at[peer], recv_sem=ag_r.at[slot],
            device_id={"head": peer}, device_id_type=MESH)

    def d_copy(peer, slot):
        return pltpu.make_async_remote_copy(
            src_ref=dsend.at[lax.div(peer, NI)], dst_ref=drecv.at[slot], send_sem=d_s.at[peer], recv_sem=d_r.at[slot],
            device_id={"seq": seq_id(me_y, peer)}, device_id_type=MESH)

    def f_copy(peer, slot):
        return pltpu.make_async_remote_copy(
            src_ref=fsend.at[peer], dst_ref=frecv.at[slot], send_sem=f_s.at[peer], recv_sem=f_r.at[slot],
            device_id={"seq": seq_id(me_y, peer)}, device_id_type=MESH)

    def y_copy(peer, slot):
        return pltpu.make_async_remote_copy(
            src_ref=ysend, dst_ref=yrecv.at[slot], send_sem=y_s.at[peer], recv_sem=y_r.at[slot],
            device_id={"seq": seq_id(peer, me_z)}, device_id_type=MESH)

    def g_copy(peer, slot):
        return pltpu.make_async_remote_copy(
            src_ref=gsend.at[peer], dst_ref=grecv.at[slot], send_sem=g_s.at[peer], recv_sem=g_r.at[slot],
            device_id={"seq": seq_id(me_y, peer)}, device_id_type=MESH)

    def s_copy(peer, slot):
        return pltpu.make_async_remote_copy(
            src_ref=srecv.at[slot], dst_ref=srecv.at[slot], send_sem=s_s.at[peer], recv_sem=s_r.at[slot],
            device_id={"head": peer}, device_id_type=MESH)

    def each(n, peer_of, action):
        @pl.loop(1, n)
        def _(r):
            action(peer_of(r))

    pl.semaphore_wait(barrier, (NH - 1) + (NZ - 1) + (NY - 1))
    each(NH, head_peer, lambda p: rs_copy(p, p, me_h).start())

    loads[2].wait()
    loads[3].wait()
    lane = lax.broadcasted_iota(jnp.int32, (T, 128), 1)
    low_lane = lane < HEAD_DIM
    rows = lax.broadcasted_iota(jnp.int32, (T, T), 0)
    cols = lax.broadcasted_iota(jnp.int32, (T, T), 1)
    causal = rows >= cols
    tri = jnp.where(causal, 1.0, 0.0).astype(BF16)
    log_decay = -(dt_v[...] * rate_v[...])
    log_decay = jnp.concatenate([log_decay, jnp.zeros((T, 128 - HEADS), F32)], axis=1)
    top = log_decay.astype(BF16)
    rest = log_decay - top.astype(F32)
    mid = rest.astype(BF16)
    low = (rest - mid.astype(F32)).astype(BF16)
    cum = ((dot(tri, low) + dot(tri, mid)) + dot(tri, top)) * LOG2E
    cum_end = cum[T - 1:T, :]
    grow = jnp.exp2(cum)
    tail = jnp.exp2(cum_end - cum)

    def spread(value, q, n):
        a = jnp.broadcast_to(value[:, 2 * q:2 * q + 1], (n, 128))
        b = jnp.broadcast_to(value[:, 2 * q + 1:2 * q + 2], (n, 128))
        return jnp.where(low_lane[:n], a, b)

    for q in range(HEADS // 2):
        at = pl.ds(128 * q, 128)
        e = spread(grow, q, T)
        expand[:, at] = e
        dsend[q // (HEADS // 4), :, pl.ds(128 * (q % (HEADS // 4)), 128)] = e[T - 1:T, :]
    each(NZ, z_peer, lambda p: d_copy(p, me_z).start())
    drecv[pl.ds(me_z, 1)] = dsend[pl.ds(lax.div(me_z, NI), 1)]

    loads[4].wait()
    dt_all = dt_v[...]
    for q in range(HEADS // 2):
        at = pl.ds(128 * q, 128)
        s = (x_v[:, at].astype(F32) * spread(dt_all, q, T)).astype(BF16)
        scl[:, at] = s
        wgt[:, at] = (spread(tail, q, T) * s.astype(F32)).astype(BF16)

    total = part[pl.ds(me_h, 1)]
    each(NH, head_peer, lambda p: rs_copy(p, p, p).wait_recv())
    rsr[pl.ds(me_h, 1)] = total
    total = rsr[0]
    for k in range(1, NH):
        total = total + rsr[k]
    agr[pl.ds(me_h, 1)] = total.astype(BF16)[None]
    each(NH, head_peer, lambda p: ag_copy(p, me_h).start())
    each(NH, head_peer, lambda p: ag_copy(p, p).wait_recv())
    projected = agr[...].reshape(T, 2 * STATE)
    b_rows = projected[:, :STATE]
    c_rows = projected[:, STATE:]
    b_cols = b_rows.astype(F32).T.astype(BF16)

    SR = STATE // NI
    for j in range(2):
        fresh = dot(b_cols, wgt[:, pl.ds(HALF * j, HALF)]).astype(BF16)
        fsend[pl.ds(NI * j, NI)] = fresh.reshape(NI, SR, HALF)
    each(NZ, z_peer, lambda p: f_copy(p, me_z).start())
    frecv[pl.ds(me_z, 1)] = fsend[pl.ds(me_z, 1)]

    loads[5].wait()
    scores = dot(c_rows, b_cols)
    M = T // 2
    tri_half = causal[:M, :M]
    s00 = jnp.where(tri_half, scores[:M, :M], 0.0)
    s10 = scores[M:, :M]
    s11 = jnp.where(tri_half, scores[M:, M:], 0.0)
    cum_rows = cum.T
    low_half = low_lane[:T]
    for q in range(HEADS // 2):
        at = pl.ds(128 * q, 128)
        mix = []
        for h in (2 * q, 2 * q + 1):
            down = jnp.broadcast_to(cum[:, h:h + 1], (T, M))
            along = cum_rows[h:h + 1, :]
            m00 = s00 * jnp.exp2(jnp.minimum(down[:M] - along[:, :M], 0.0))
            m10 = s10 * jnp.exp2(down[M:] - along[:, :M])
            m11 = s11 * jnp.exp2(jnp.minimum(down[M:] - along[:, M:], 0.0))
            mix.append((m00.astype(BF16), jnp.concatenate([m10.astype(BF16), m11.astype(BF16)], axis=1)))
        s = scl[:, at]
        zero = jnp.zeros_like(s)
        sa = jnp.where(low_half, s, zero)
        sb = jnp.where(low_half, zero, s)
        upper = dot(jnp.concatenate([mix[0][0], mix[1][0]], axis=1), jnp.concatenate([sa[:M], sb[:M]], axis=0))
        lower = dot(mix[0][1], sa) + dot(mix[1][1], sb)
        v = g_v[:, at].astype(F32)
        silu = v / (1.0 + jnp.exp(-v))
        fac[:, at] = expand[:, at] * silu
        acc[:M, at] = upper * silu[:M]
        acc[M:, at] = lower * silu[M:]

    each(NZ, z_peer, lambda p: d_copy(p, p).wait_recv())
    each(NZ, z_peer, lambda p: f_copy(p, p).wait_recv())
    carry = frecv[0].astype(F32)
    span = drecv[0]
    for k in range(1, NZ):
        carry = drecv[k] * carry + frecv[k].astype(F32)
        span = drecv[k] * span
    ysend[:SR] = carry
    ysend[SR:] = jnp.broadcast_to(span, (8, HALF))
    each(NY, y_peer, lambda p: y_copy(p, me_y).start())
    yrecv[pl.ds(me_y, 1)] = ysend[...][None]
    each(NY, y_peer, lambda p: y_copy(p, p).wait_recv())
    carry = jnp.zeros((SR, HALF), F32)
    for k in range(NY - 1):
        later = yrecv[k, SR:SR + 1] * carry + yrecv[k, :SR]
        carry = jnp.where(k < me_y, later, carry)
    for k in range(NZ):
        gsend[k] = carry.astype(BF16)
        carry = drecv[k] * carry + frecv[k].astype(F32)
    each(NZ, z_peer, lambda p: g_copy(p, me_z).start())
    grecv[pl.ds(me_z, 1)] = gsend[pl.ds(me_z, 1)]
    each(NZ, z_peer, lambda p: g_copy(p, p).wait_recv())

    squares = jnp.zeros((T, 128), F32)
    for j in range(2):
        entering = grecv[pl.ds(NI * j, NI)].reshape(STATE, HALF)
        at = pl.ds(HALF * j, HALF)
        gated = acc[:, at] + dot(c_rows, entering) * fac[:, at]
        gated_v[:, at] = gated
        sq = gated * gated
        for i in range(HALF // 128):
            squares = squares + sq[:, 128 * i:128 * i + 128]
    srecv[pl.ds(me_h, 1)] = jnp.sum(squares.T, axis=0, keepdims=True)[None]
    each(NH, head_peer, lambda p: s_copy(p, me_h).start())
    each(NH, head_peer, lambda p: s_copy(p, p).wait_recv())
    mean = srecv[0]
    for k in range(1, NH):
        mean = mean + srecv[k]
    mean = mean / (NH * COLS)
    scale = lax.rsqrt(jnp.broadcast_to(mean, (128, T)) + 1e-05).T
    loads[6].wait()
    for q in range(HEADS // 2):
        at = pl.ds(128 * q, 128)
        out[:, at] = (gated_v[:, at] * scale * gain_v[:, at]).astype(BF16)

    each(NH, head_peer, lambda p: rs_copy(p, p, me_h).wait_send())
    each(NH, head_peer, lambda p: ag_copy(p, me_h).wait_send())
    each(NH, head_peer, lambda p: s_copy(p, me_h).wait_send())
    each(NZ, z_peer, lambda p: d_copy(p, me_z).wait_send())
    each(NZ, z_peer, lambda p: f_copy(p, me_z).wait_send())
    each(NZ, z_peer, lambda p: g_copy(p, me_z).wait_send())
    each(NY, y_peer, lambda p: y_copy(p, me_y).wait_send())


def shards(NH, NY, NZ, hidden_in, proj_weight, head_input, gate_input, step_size, decay_rate, norm_gain):
    KD = hidden_in.shape[1]
    RB = T // NH
    SR = STATE // (NZ // 2)
    any_space = pl.BlockSpec(memory_space=pl.ANY)
    vm, dma = pltpu.VMEM, pltpu.SemaphoreType.DMA
    return pl.pallas_call(
        functools.partial(kernel, NH, NY, NZ),
        name="layer",
        out_shape=jax.ShapeDtypeStruct((T, COLS), BF16),
        in_specs=[any_space] * 7,
        out_specs=pl.BlockSpec(memory_space=pltpu.VMEM),
        scratch_shapes=[
            vm((T, KD), BF16), vm((KD, 2 * STATE), BF16), vm((T, COLS), BF16), vm((T, COLS), BF16),
            vm((T, HEADS), F32), vm((1, HEADS), F32), vm((1, COLS), F32), dma((7,)),
            vm((NH, RB, 2 * STATE), F32), vm((NH, RB, 2 * STATE), F32), vm((NH, RB, 2 * STATE), BF16),
            vm((T, COLS), BF16), vm((T, COLS), BF16), vm((T, COLS), F32),
            vm((NZ, SR, HALF), BF16), vm((NZ, SR, HALF), BF16), vm((2, 1, HALF), F32), vm((NZ, 1, HALF), F32),
            vm((SR + 8, HALF), F32), vm((NY, SR + 8, HALF), F32), vm((NZ, SR, HALF), BF16), vm((NZ, SR, HALF), BF16),
            vm((T, COLS), F32), vm((T, COLS), F32), vm((T, COLS), F32), vm((NH, 1, T), F32),
            dma((NH,)), dma((NH,)), dma((NH,)), dma((NH,)), dma((NZ,)), dma((NZ,)), dma((NZ,)), dma((NZ,)),
            dma((NY,)), dma((NY,)), dma((NZ,)), dma((NZ,)), dma((NH,)), dma((NH,)),
        ],
        compiler_params=pltpu.CompilerParams(collective_id=0, has_side_effects=True),
    )(hidden_in, proj_weight, head_input, gate_input, step_size, decay_rate.reshape(1, HEADS), norm_gain.reshape(1, COLS))


def solution(mesh):
    NZ = 16
    NY = mesh.shape["seq"] // NZ
    NH = mesh.shape["head"]
    in_specs = (
        P("seq", "head"), P(), P("seq", "head"), P("seq", "head"), P("seq", "head"), P("head"), P("head"),
    )
    return jax.shard_map(
        functools.partial(shards, NH, NY, NZ), mesh=mesh, in_specs=in_specs, out_specs=P("seq", "head"), check_vma=False)
```

```python
import functools
import math

import jax
import jax.numpy as jnp
from jax import lax
from jax.experimental import pallas as pl
from jax.experimental.pallas import tpu as pltpu
from jax.sharding import PartitionSpec as P

MESH = pl.DeviceIdType.MESH
F32, BF16 = jnp.float32, jnp.bfloat16
T = 256
HEADS = 16
HEAD_DIM = 64
STATE = 128
COLS = HEADS * HEAD_DIM
HALF = COLS // 2
CW = HALF // 2
LOG2E = math.log2(math.e)


def dot(a, b):
    return jnp.dot(a, b, preferred_element_type=F32)


def kernel(
    NH, NY, NZ,
    hid, w, x, g, dt, rate, gain, out,
    hid_v, w_v, x_v, g_v, dt_v, rate_v, gain_v, in_sem,
    part, rsr, agr, scl, wgt, expand,
    fsend, frecv, dsend, drecv, ysend, yrecv, gsend, grecv,
    acc, fac, gated_v, srecv,
    rs_s, rs_r, ag_s, ag_r, d_s, d_r, f_s, f_r, y_s, y_r, g_s, g_r, s_s, s_r, from_left, from_right,
):
    KD = hid_v.shape[1]
    RB = T // NH
    NI = NZ // 2
    SR = STATE // NI
    me_h = lax.axis_index("head")
    seq = lax.axis_index("seq")
    me_z = lax.rem(seq, NZ)
    me_y = lax.div(seq, NZ)

    def head_peer(r):
        return lax.rem(me_h + r, NH)

    def far_first(k):
        off = lax.div(k, 2)
        return NZ // 2 + jnp.where(lax.rem(k, 2) == 1, off, -off)

    def z_peer(k):
        return lax.rem(me_z + far_first(k), NZ)

    def y_peer(r):
        return lax.rem(me_y + r, NY)

    def seq_id(y, z):
        return y * NZ + z

    right = {"seq": seq_id(me_y, lax.rem(me_z + 1, NZ))}
    left = {"seq": seq_id(me_y, lax.rem(me_z + NZ - 1, NZ))}

    def each(n, peer_of, action):
        @pl.loop(1, n)
        def _(r):
            action(peer_of(r))

    def signal(sem, device):
        pl.semaphore_signal(sem, inc=1, device_id=device, device_id_type=MESH)

    barrier = pltpu.get_barrier_semaphore()
    signal(barrier, right)
    signal(barrier, left)
    each(NH, head_peer, lambda p: signal(barrier, {"head": p}))
    each(NY, y_peer, lambda p: signal(barrier, {"seq": seq_id(p, me_z)}))

    loads = [
        pltpu.make_async_copy(hid, hid_v, in_sem.at[0]),
        pltpu.make_async_copy(w.at[pl.ds(pl.multiple_of(me_h * KD, KD), KD)], w_v, in_sem.at[1]),
        pltpu.make_async_copy(dt, dt_v, in_sem.at[2]),
        pltpu.make_async_copy(rate, rate_v, in_sem.at[3]),
        pltpu.make_async_copy(x, x_v, in_sem.at[4]),
        pltpu.make_async_copy(g, g_v, in_sem.at[5]),
        pltpu.make_async_copy(gain, gain_v, in_sem.at[6]),
    ]
    for load in loads:
        load.start()
    loads[0].wait()
    loads[1].wait()
    own = dot(hid_v[...], w_v[...])
    for m in range(2):
        part[m] = own[:, STATE * m:STATE * m + STATE].reshape(NH, RB, STATE)

    def remote(src, dst, send_sem, recv_sem, device):
        return pltpu.make_async_remote_copy(
            src_ref=src, dst_ref=dst, send_sem=send_sem, recv_sem=recv_sem, device_id=device, device_id_type=MESH)

    def rs_copy(m, peer, slot):
        return remote(part.at[m, peer], rsr.at[m, slot], rs_s.at[m, peer], rs_r.at[m, slot], {"head": peer})

    def ag_copy(m, peer, slot):
        return remote(agr.at[m, slot], agr.at[m, slot], ag_s.at[m, peer], ag_r.at[m, slot], {"head": peer})

    def d_copy(peer, slot):
        return remote(dsend.at[lax.div(peer, NI)], drecv.at[slot], d_s.at[peer], d_r.at[slot], {"seq": seq_id(me_y, peer)})

    def f_copy(c, peer, slot):
        return remote(fsend.at[c, peer], frecv.at[c, slot], f_s.at[c, peer], f_r.at[c, slot], {"seq": seq_id(me_y, peer)})

    def y_copy(c, peer, slot):
        return remote(ysend.at[c], yrecv.at[c, slot], y_s.at[c, peer], y_r.at[c, slot], {"seq": seq_id(peer, me_z)})

    def g_copy(c, peer, slot):
        return remote(gsend.at[c, peer], grecv.at[c, slot], g_s.at[c, peer], g_r.at[c, slot], {"seq": seq_id(me_y, peer)})

    def s_copy(peer, slot):
        return remote(srecv.at[slot], srecv.at[slot], s_s.at[peer], s_r.at[slot], {"head": peer})

    pl.semaphore_wait(barrier, (NH - 1) + (NY - 1) + 2)
    for m in range(2):
        each(NH, head_peer, lambda p: rs_copy(m, p, me_h).start())

    def relay():
        signal(from_left, right)
        signal(from_right, left)
        pl.semaphore_wait(from_left, 1)
        pl.semaphore_wait(from_right, 1)

    loads[2].wait()
    loads[3].wait()
    lane = lax.broadcasted_iota(jnp.int32, (T, 128), 1)
    low_lane = lane < HEAD_DIM
    rows = lax.broadcasted_iota(jnp.int32, (T, T), 0)
    cols = lax.broadcasted_iota(jnp.int32, (T, T), 1)
    causal = rows >= cols
    tri = jnp.where(causal, 1.0, 0.0).astype(BF16)
    dt_all = jnp.concatenate([dt_v[...], jnp.zeros((128 - HEADS, T), F32)], axis=0).T
    rate_all = jnp.concatenate([rate_v[...], jnp.zeros((1, 128 - HEADS), F32)], axis=1)
    log_decay = -(dt_all * rate_all)
    top = log_decay.astype(BF16)
    rest = log_decay - top.astype(F32)
    mid = rest.astype(BF16)
    low = (rest - mid.astype(F32)).astype(BF16)
    cum = ((dot(tri, low) + dot(tri, mid)) + dot(tri, top)) * LOG2E
    cum_end = cum[T - 1:T, :]
    grow = jnp.exp2(cum)
    tail = jnp.exp2(cum_end - cum)

    def spread(value, q):
        a = jnp.broadcast_to(value[:, 2 * q:2 * q + 1], (T, 128))
        b = jnp.broadcast_to(value[:, 2 * q + 1:2 * q + 2], (T, 128))
        return jnp.where(low_lane, a, b)

    hops = NZ // 2 - 1
    for q in range(HEADS // 2):
        if q < hops:
            relay()
        at = pl.ds(128 * q, 128)
        e = spread(grow, q)
        expand[:, at] = e
        dsend[(q % 4) // 2, q // 4, :, pl.ds(128 * (q % 2), 128)] = e[T - 1:T, :]

    loads[4].wait()
    for q in range(HEADS // 2):
        at = pl.ds(128 * q, 128)
        s = (x_v[:, at].astype(F32) * spread(dt_all, q)).astype(BF16)
        scl[:, at] = s
        wgt[:, at] = (spread(tail, q) * s.astype(F32)).astype(BF16)
    each(NZ, z_peer, lambda p: d_copy(p, me_z).start())
    drecv[pl.ds(me_z, 1)] = dsend[pl.ds(lax.div(me_z, NI), 1)]

    for m in range(2):
        rsr[m, pl.ds(me_h, 1)] = part[m, pl.ds(me_h, 1)]
        each(NH, head_peer, lambda p: rs_copy(m, p, p).wait_recv())
        total = rsr[m, 0]
        for k in range(1, NH):
            total = total + rsr[m, k]
        agr[m, pl.ds(me_h, 1)] = total.astype(BF16)[None]
        each(NH, head_peer, lambda p: ag_copy(m, p, me_h).start())
    each(NH, head_peer, lambda p: ag_copy(0, p, p).wait_recv())
    b_cols = agr[0].reshape(T, STATE).astype(F32).T.astype(BF16)

    for c in range(2):
        for j in range(2):
            fresh = dot(b_cols, wgt[:, pl.ds(HALF * c + CW * j, CW)]).astype(BF16)
            fsend[c, pl.ds(NI * j, NI)] = fresh.reshape(NI, SR, CW)
        each(NZ, z_peer, lambda p: f_copy(c, p, me_z).start())
        frecv[c, pl.ds(me_z, 1)] = fsend[c, pl.ds(me_z, 1)]

    each(NH, head_peer, lambda p: ag_copy(1, p, p).wait_recv())
    c_rows = agr[1].reshape(T, STATE)
    loads[5].wait()
    scores = dot(c_rows, b_cols)
    M = T // 2
    tri_half = causal[:M, :M]
    s00 = jnp.where(tri_half, scores[:M, :M], 0.0)
    s10 = scores[M:, :M]
    s11 = jnp.where(tri_half, scores[M:, M:], 0.0)
    cum_rows = cum.T
    for q in range(HEADS // 2):
        at = pl.ds(128 * q, 128)
        mix = []
        for h in (2 * q, 2 * q + 1):
            down = jnp.broadcast_to(cum[:, h:h + 1], (T, M))
            along = cum_rows[h:h + 1, :]
            m00 = s00 * jnp.exp2(jnp.minimum(down[:M] - along[:, :M], 0.0))
            m10 = s10 * jnp.exp2(down[M:] - along[:, :M])
            m11 = s11 * jnp.exp2(jnp.minimum(down[M:] - along[:, M:], 0.0))
            mix.append((m00.astype(BF16), jnp.concatenate([m10.astype(BF16), m11.astype(BF16)], axis=1)))
        s = scl[:, at]
        zero = jnp.zeros_like(s)
        sa = jnp.where(low_lane, s, zero)
        sb = jnp.where(low_lane, zero, s)
        upper = dot(jnp.concatenate([mix[0][0], mix[1][0]], axis=1), jnp.concatenate([sa[:M], sb[:M]], axis=0))
        lower = dot(mix[0][1], sa) + dot(mix[1][1], sb)
        v = g_v[:, at].astype(F32)
        silu = v / (1.0 + jnp.exp(-v))
        fac[:, at] = expand[:, at] * silu
        acc[:M, at] = upper * silu[:M]
        acc[M:, at] = lower * silu[M:]

    each(NZ, z_peer, lambda p: d_copy(p, p).wait_recv())
    for c in range(2):
        each(NZ, z_peer, lambda p: f_copy(c, p, p).wait_recv())
        carry = frecv[c, 0].astype(F32)
        span = drecv[0, c]
        for k in range(1, NZ):
            carry = drecv[k, c] * carry + frecv[c, k].astype(F32)
            span = drecv[k, c] * span
        ysend[c, :SR] = carry
        ysend[c, SR:] = jnp.broadcast_to(span, (8, CW))
        each(NY, y_peer, lambda p: y_copy(c, p, me_y).start())
        yrecv[c, pl.ds(me_y, 1)] = ysend[c][None]
    for c in range(2):
        each(NY, y_peer, lambda p: y_copy(c, p, p).wait_recv())
        carry = jnp.zeros((SR, CW), F32)
        for k in range(NY - 1):
            later = yrecv[c, k, SR:SR + 1] * carry + yrecv[c, k, :SR]
            carry = jnp.where(k < me_y, later, carry)
        for k in range(NZ):
            gsend[c, k] = carry.astype(BF16)
            carry = drecv[k, c] * carry + frecv[c, k].astype(F32)
        each(NZ, z_peer, lambda p: g_copy(c, p, me_z).start())
        grecv[c, pl.ds(me_z, 1)] = gsend[c, pl.ds(me_z, 1)]

    squares = jnp.zeros((T, 128), F32)
    for c in range(2):
        each(NZ, z_peer, lambda p: g_copy(c, p, p).wait_recv())
        for j in range(2):
            entering = grecv[c, pl.ds(NI * j, NI)].reshape(STATE, CW)
            at = pl.ds(HALF * c + CW * j, CW)
            gated = acc[:, at] + dot(c_rows, entering) * fac[:, at]
            gated_v[:, at] = gated
            sq = gated * gated
            for i in range(CW // 128):
                squares = squares + sq[:, 128 * i:128 * i + 128]
    srecv[pl.ds(me_h, 1)] = jnp.sum(squares.T, axis=0, keepdims=True)[None]
    each(NH, head_peer, lambda p: s_copy(p, me_h).start())
    each(NH, head_peer, lambda p: s_copy(p, p).wait_recv())
    mean = srecv[0]
    for k in range(1, NH):
        mean = mean + srecv[k]
    mean = mean / (NH * COLS)
    scale = lax.rsqrt(jnp.broadcast_to(mean, (128, T)) + 1e-05).T
    loads[6].wait()
    for q in range(HEADS // 2):
        at = pl.ds(128 * q, 128)
        out[:, at] = (gated_v[:, at] * scale * gain_v[:, at]).astype(BF16)

    for m in range(2):
        each(NH, head_peer, lambda p: rs_copy(m, p, me_h).wait_send())
        each(NH, head_peer, lambda p: ag_copy(m, p, me_h).wait_send())
    each(NH, head_peer, lambda p: s_copy(p, me_h).wait_send())
    each(NZ, z_peer, lambda p: d_copy(p, me_z).wait_send())
    for c in range(2):
        each(NZ, z_peer, lambda p: f_copy(c, p, me_z).wait_send())
        each(NZ, z_peer, lambda p: g_copy(c, p, me_z).wait_send())
        each(NY, y_peer, lambda p: y_copy(c, p, me_y).wait_send())


def shards(NH, NY, NZ, hidden_in, proj_weight, head_input, gate_input, step_size, decay_rate, norm_gain):
    KD = hidden_in.shape[1]
    RB = T // NH
    SR = STATE // (NZ // 2)
    operands = (hidden_in, proj_weight, head_input, gate_input, step_size.T, decay_rate.reshape(1, HEADS), norm_gain.reshape(1, COLS))
    in_hbm = pl.BlockSpec(memory_space=pltpu.HBM)
    vm, dma = pltpu.VMEM, pltpu.SemaphoreType.DMA
    return pl.pallas_call(
        functools.partial(kernel, NH, NY, NZ),
        name="layer",
        out_shape=jax.ShapeDtypeStruct((T, COLS), BF16),
        in_specs=[in_hbm] * 7,
        out_specs=pl.BlockSpec(memory_space=pltpu.VMEM),
        scratch_shapes=[
            vm((T, KD), BF16), vm((KD, 2 * STATE), BF16), vm((T, COLS), BF16), vm((T, COLS), BF16),
            vm((HEADS, T), F32), vm((1, HEADS), F32), vm((1, COLS), F32), dma((7,)),
            vm((2, NH, RB, STATE), F32), vm((2, NH, RB, STATE), F32), vm((2, NH, RB, STATE), BF16),
            vm((T, COLS), BF16), vm((T, COLS), BF16), vm((T, COLS), F32),
            vm((2, NZ, SR, CW), BF16), vm((2, NZ, SR, CW), BF16), vm((2, 2, 1, CW), F32), vm((NZ, 2, 1, CW), F32),
            vm((2, SR + 8, CW), F32), vm((2, NY, SR + 8, CW), F32), vm((2, NZ, SR, CW), BF16), vm((2, NZ, SR, CW), BF16),
            vm((T, COLS), F32), vm((T, COLS), F32), vm((T, COLS), F32), vm((NH, 1, T), F32),
            dma((2, NH)), dma((2, NH)), dma((2, NH)), dma((2, NH)), dma((NZ,)), dma((NZ,)), dma((2, NZ)), dma((2, NZ)),
            dma((2, NY)), dma((2, NY)), dma((2, NZ)), dma((2, NZ)), dma((NH,)), dma((NH,)),
            pltpu.SemaphoreType.REGULAR, pltpu.SemaphoreType.REGULAR,
        ],
        compiler_params=pltpu.CompilerParams(collective_id=0, has_side_effects=True, vmem_limit_bytes=20 * 2**20),
    )(*(pltpu.with_memory_space_constraint(operand, pltpu.HBM) for operand in operands))


def solution(mesh):
    NZ = 16
    NY = mesh.shape["seq"] // NZ
    NH = mesh.shape["head"]
    in_specs = (
        P("seq", "head"), P(), P("seq", "head"), P("seq", "head"), P("seq", "head"), P("head"), P("head"),
    )
    return jax.shard_map(
        functools.partial(shards, NH, NY, NZ), mesh=mesh, in_specs=in_specs, out_specs=P("seq", "head"), check_vma=False)
```

```python
import functools
import math

import jax
import jax.numpy as jnp
from jax import lax
from jax.experimental import pallas as pl
from jax.experimental.pallas import tpu as pltpu
from jax.sharding import PartitionSpec as P

MESH = pl.DeviceIdType.MESH
F32, BF16 = jnp.float32, jnp.bfloat16
T = 256
HEADS = 16
HEAD_DIM = 64
STATE = 128
COLS = HEADS * HEAD_DIM
HALF = COLS // 2
CW = HALF // 2
LOG2E = math.log2(math.e)


def dot(a, b):
    return jnp.dot(a, b, preferred_element_type=F32)


def kernel(
    NH, NY, NZ,
    hid, w, x, g, dt, rate, gain, out,
    hid_v, w_v, x_v, g_v, dt_v, rate_v, gain_v, in_sem,
    part, rsr, agr, scl, wgt, expand,
    fsend, frecv, dsend, drecv, ysend, yrecv, gsend, grecv,
    acc, fac, gated_v, srecv,
    rs_s, rs_r, ag_s, ag_r, d_s, d_r, f_s, f_r, y_s, y_r, g_s, g_r, s_s, s_r,
):
    KD = hid_v.shape[1]
    RB = T // NH
    NI = NZ // 2
    SR = STATE // NI
    me_h = lax.axis_index("head")
    seq = lax.axis_index("seq")
    me_z = lax.rem(seq, NZ)
    me_y = lax.div(seq, NZ)

    def head_peer(r):
        return lax.rem(me_h + r, NH)

    def far_first(k):
        off = lax.div(k, 2)
        return NZ // 2 + jnp.where(lax.rem(k, 2) == 1, off, -off)

    def z_peer(k):
        return lax.rem(me_z + far_first(k), NZ)

    def y_peer(r):
        return lax.rem(me_y + r, NY)

    def seq_id(y, z):
        return y * NZ + z

    def each(n, peer_of, action):
        @pl.loop(1, n)
        def _(r):
            action(peer_of(r))

    def signal(sem, device):
        pl.semaphore_signal(sem, inc=1, device_id=device, device_id_type=MESH)

    barrier = pltpu.get_barrier_semaphore()
    each(NZ, z_peer, lambda p: signal(barrier, {"seq": seq_id(me_y, p)}))
    each(NY, y_peer, lambda p: signal(barrier, {"seq": seq_id(p, me_z)}))
    each(NH, head_peer, lambda p: signal(barrier, {"head": p}))

    loads = [
        pltpu.make_async_copy(hid, hid_v, in_sem.at[0]),
        pltpu.make_async_copy(w.at[pl.ds(pl.multiple_of(me_h * KD, KD), KD)], w_v, in_sem.at[1]),
        pltpu.make_async_copy(dt, dt_v, in_sem.at[2]),
        pltpu.make_async_copy(rate, rate_v, in_sem.at[3]),
        pltpu.make_async_copy(x, x_v, in_sem.at[4]),
        pltpu.make_async_copy(g, g_v, in_sem.at[5]),
        pltpu.make_async_copy(gain, gain_v, in_sem.at[6]),
    ]
    for load in loads:
        load.start()
    loads[0].wait()
    loads[1].wait()
    own = dot(hid_v[...], w_v[...])
    for m in range(2):
        part[m] = own[:, STATE * m:STATE * m + STATE].reshape(NH, RB, STATE)

    def remote(src, dst, send_sem, recv_sem, device):
        return pltpu.make_async_remote_copy(
            src_ref=src, dst_ref=dst, send_sem=send_sem, recv_sem=recv_sem, device_id=device, device_id_type=MESH)

    def rs_copy(m, peer, slot):
        return remote(part.at[m, peer], rsr.at[m, slot], rs_s.at[m, peer], rs_r.at[m, slot], {"head": peer})

    def ag_copy(m, peer, slot):
        return remote(agr.at[m, slot], agr.at[m, slot], ag_s.at[m, peer], ag_r.at[m, slot], {"head": peer})

    def d_copy(peer, slot):
        return remote(dsend.at[lax.div(peer, NI)], drecv.at[slot], d_s.at[peer], d_r.at[slot], {"seq": seq_id(me_y, peer)})

    def f_copy(c, peer, slot):
        return remote(fsend.at[c, peer], frecv.at[c, slot], f_s.at[c, peer], f_r.at[c, slot], {"seq": seq_id(me_y, peer)})

    def y_copy(c, peer, slot):
        return remote(ysend.at[c], yrecv.at[c, slot], y_s.at[c, peer], y_r.at[c, slot], {"seq": seq_id(peer, me_z)})

    def g_copy(c, peer, slot):
        return remote(gsend.at[c, peer], grecv.at[c, slot], g_s.at[c, peer], g_r.at[c, slot], {"seq": seq_id(me_y, peer)})

    def s_copy(peer, slot):
        return remote(srecv.at[slot], srecv.at[slot], s_s.at[peer], s_r.at[slot], {"head": peer})

    pl.semaphore_wait(barrier, (NH - 1) + (NY - 1) + (NZ - 1))
    for m in range(2):
        each(NH, head_peer, lambda p: rs_copy(m, p, me_h).start())

    loads[2].wait()
    loads[3].wait()
    lane = lax.broadcasted_iota(jnp.int32, (T, 128), 1)
    low_lane = lane < HEAD_DIM
    rows = lax.broadcasted_iota(jnp.int32, (T, T), 0)
    cols = lax.broadcasted_iota(jnp.int32, (T, T), 1)
    causal = rows >= cols
    tri = jnp.where(causal, 1.0, 0.0).astype(BF16)
    dt_all = jnp.concatenate([dt_v[...], jnp.zeros((128 - HEADS, T), F32)], axis=0).T
    rate_all = jnp.concatenate([rate_v[...], jnp.zeros((1, 128 - HEADS), F32)], axis=1)
    log_decay = -(dt_all * rate_all)
    top = log_decay.astype(BF16)
    rest = log_decay - top.astype(F32)
    mid = rest.astype(BF16)
    low = (rest - mid.astype(F32)).astype(BF16)
    cum = ((dot(tri, low) + dot(tri, mid)) + dot(tri, top)) * LOG2E
    cum_end = cum[T - 1:T, :]
    grow = jnp.exp2(cum)
    tail = jnp.exp2(cum_end - cum)

    def spread(value, q):
        a = jnp.broadcast_to(value[:, 2 * q:2 * q + 1], (T, 128))
        b = jnp.broadcast_to(value[:, 2 * q + 1:2 * q + 2], (T, 128))
        return jnp.where(low_lane, a, b)

    for q in range(HEADS // 2):
        at = pl.ds(128 * q, 128)
        e = spread(grow, q)
        expand[:, at] = e
        dsend[(q % 4) // 2, q // 4, :, pl.ds(128 * (q % 2), 128)] = e[T - 1:T, :]

    loads[4].wait()
    for q in range(HEADS // 2):
        at = pl.ds(128 * q, 128)
        s = (x_v[:, at].astype(F32) * spread(dt_all, q)).astype(BF16)
        scl[:, at] = s
        wgt[:, at] = (spread(tail, q) * s.astype(F32)).astype(BF16)
    each(NZ, z_peer, lambda p: d_copy(p, me_z).start())
    drecv[pl.ds(me_z, 1)] = dsend[pl.ds(lax.div(me_z, NI), 1)]

    for m in range(2):
        rsr[m, pl.ds(me_h, 1)] = part[m, pl.ds(me_h, 1)]
        each(NH, head_peer, lambda p: rs_copy(m, p, p).wait_recv())
        total = rsr[m, 0]
        for k in range(1, NH):
            total = total + rsr[m, k]
        agr[m, pl.ds(me_h, 1)] = total.astype(BF16)[None]
        each(NH, head_peer, lambda p: ag_copy(m, p, me_h).start())
    each(NH, head_peer, lambda p: ag_copy(0, p, p).wait_recv())
    b_cols = agr[0].reshape(T, STATE).astype(F32).T.astype(BF16)

    for c in range(2):
        for j in range(2):
            fresh = dot(b_cols, wgt[:, pl.ds(HALF * c + CW * j, CW)]).astype(BF16)
            fsend[c, pl.ds(NI * j, NI)] = fresh.reshape(NI, SR, CW)
        each(NZ, z_peer, lambda p: f_copy(c, p, me_z).start())
        frecv[c, pl.ds(me_z, 1)] = fsend[c, pl.ds(me_z, 1)]

    each(NH, head_peer, lambda p: ag_copy(1, p, p).wait_recv())
    c_rows = agr[1].reshape(T, STATE)
    loads[5].wait()
    scores = dot(c_rows, b_cols)
    M = T // 2
    tri_half = causal[:M, :M]
    s00 = jnp.where(tri_half, scores[:M, :M], 0.0)
    s10 = scores[M:, :M]
    s11 = jnp.where(tri_half, scores[M:, M:], 0.0)
    cum_rows = cum.T
    for q in range(HEADS // 2):
        at = pl.ds(128 * q, 128)
        mix = []
        for h in (2 * q, 2 * q + 1):
            down = jnp.broadcast_to(cum[:, h:h + 1], (T, M))
            along = cum_rows[h:h + 1, :]
            m00 = s00 * jnp.exp2(jnp.minimum(down[:M] - along[:, :M], 0.0))
            m10 = s10 * jnp.exp2(down[M:] - along[:, :M])
            m11 = s11 * jnp.exp2(jnp.minimum(down[M:] - along[:, M:], 0.0))
            mix.append((m00.astype(BF16), jnp.concatenate([m10.astype(BF16), m11.astype(BF16)], axis=1)))
        s = scl[:, at]
        zero = jnp.zeros_like(s)
        sa = jnp.where(low_lane, s, zero)
        sb = jnp.where(low_lane, zero, s)
        upper = dot(jnp.concatenate([mix[0][0], mix[1][0]], axis=1), jnp.concatenate([sa[:M], sb[:M]], axis=0))
        lower = dot(mix[0][1], sa) + dot(mix[1][1], sb)
        v = g_v[:, at].astype(F32)
        silu = v / (1.0 + jnp.exp(-v))
        fac[:, at] = expand[:, at] * silu
        acc[:M, at] = upper * silu[:M]
        acc[M:, at] = lower * silu[M:]

    each(NZ, z_peer, lambda p: d_copy(p, p).wait_recv())
    for c in range(2):
        each(NZ, z_peer, lambda p: f_copy(c, p, p).wait_recv())
        carry = frecv[c, 0].astype(F32)
        span = drecv[0, c]
        for k in range(1, NZ):
            carry = drecv[k, c] * carry + frecv[c, k].astype(F32)
            span = drecv[k, c] * span
        ysend[c, :SR] = carry
        ysend[c, SR:] = jnp.broadcast_to(span, (8, CW))
        each(NY, y_peer, lambda p: y_copy(c, p, me_y).start())
        yrecv[c, pl.ds(me_y, 1)] = ysend[c][None]
    for c in range(2):
        each(NY, y_peer, lambda p: y_copy(c, p, p).wait_recv())
        carry = jnp.zeros((SR, CW), F32)
        for k in range(NY - 1):
            later = yrecv[c, k, SR:SR + 1] * carry + yrecv[c, k, :SR]
            carry = jnp.where(k < me_y, later, carry)
        for k in range(NZ):
            gsend[c, k] = carry.astype(BF16)
            carry = drecv[k, c] * carry + frecv[c, k].astype(F32)
        each(NZ, z_peer, lambda p: g_copy(c, p, me_z).start())
        grecv[c, pl.ds(me_z, 1)] = gsend[c, pl.ds(me_z, 1)]

    squares = jnp.zeros((T, 128), F32)
    for c in range(2):
        each(NZ, z_peer, lambda p: g_copy(c, p, p).wait_recv())
        for j in range(2):
            entering = grecv[c, pl.ds(NI * j, NI)].reshape(STATE, CW)
            at = pl.ds(HALF * c + CW * j, CW)
            gated = acc[:, at] + dot(c_rows, entering) * fac[:, at]
            gated_v[:, at] = gated
            sq = gated * gated
            for i in range(CW // 128):
                squares = squares + sq[:, 128 * i:128 * i + 128]
    srecv[pl.ds(me_h, 1)] = jnp.sum(squares.T, axis=0, keepdims=True)[None]
    each(NH, head_peer, lambda p: s_copy(p, me_h).start())
    each(NH, head_peer, lambda p: s_copy(p, p).wait_recv())
    mean = srecv[0]
    for k in range(1, NH):
        mean = mean + srecv[k]
    mean = mean / (NH * COLS)
    scale = lax.rsqrt(jnp.broadcast_to(mean, (128, T)) + 1e-05).T
    loads[6].wait()
    for q in range(HEADS // 2):
        at = pl.ds(128 * q, 128)
        out[:, at] = (gated_v[:, at] * scale * gain_v[:, at]).astype(BF16)

    for m in range(2):
        each(NH, head_peer, lambda p: rs_copy(m, p, me_h).wait_send())
        each(NH, head_peer, lambda p: ag_copy(m, p, me_h).wait_send())
    each(NH, head_peer, lambda p: s_copy(p, me_h).wait_send())
    each(NZ, z_peer, lambda p: d_copy(p, me_z).wait_send())
    for c in range(2):
        each(NZ, z_peer, lambda p: f_copy(c, p, me_z).wait_send())
        each(NZ, z_peer, lambda p: g_copy(c, p, me_z).wait_send())
        each(NY, y_peer, lambda p: y_copy(c, p, me_y).wait_send())


def shards(NH, NY, NZ, hidden_in, proj_weight, head_input, gate_input, step_size, decay_rate, norm_gain):
    KD = hidden_in.shape[1]
    RB = T // NH
    SR = STATE // (NZ // 2)
    operands = (hidden_in, proj_weight, head_input, gate_input, step_size.T, decay_rate.reshape(1, HEADS), norm_gain.reshape(1, COLS))
    in_hbm = pl.BlockSpec(memory_space=pltpu.HBM)
    vm, dma = pltpu.VMEM, pltpu.SemaphoreType.DMA
    return pl.pallas_call(
        functools.partial(kernel, NH, NY, NZ),
        name="layer",
        out_shape=jax.ShapeDtypeStruct((T, COLS), BF16),
        in_specs=[in_hbm] * 7,
        out_specs=pl.BlockSpec(memory_space=pltpu.VMEM),
        scratch_shapes=[
            vm((T, KD), BF16), vm((KD, 2 * STATE), BF16), vm((T, COLS), BF16), vm((T, COLS), BF16),
            vm((HEADS, T), F32), vm((1, HEADS), F32), vm((1, COLS), F32), dma((7,)),
            vm((2, NH, RB, STATE), F32), vm((2, NH, RB, STATE), F32), vm((2, NH, RB, STATE), BF16),
            vm((T, COLS), BF16), vm((T, COLS), BF16), vm((T, COLS), F32),
            vm((2, NZ, SR, CW), BF16), vm((2, NZ, SR, CW), BF16), vm((2, 2, 1, CW), F32), vm((NZ, 2, 1, CW), F32),
            vm((2, SR + 8, CW), F32), vm((2, NY, SR + 8, CW), F32), vm((2, NZ, SR, CW), BF16), vm((2, NZ, SR, CW), BF16),
            vm((T, COLS), F32), vm((T, COLS), F32), vm((T, COLS), F32), vm((NH, 1, T), F32),
            dma((2, NH)), dma((2, NH)), dma((2, NH)), dma((2, NH)), dma((NZ,)), dma((NZ,)), dma((2, NZ)), dma((2, NZ)),
            dma((2, NY)), dma((2, NY)), dma((2, NZ)), dma((2, NZ)), dma((NH,)), dma((NH,)),
        ],
        compiler_params=pltpu.CompilerParams(collective_id=0, has_side_effects=True, vmem_limit_bytes=20 * 2**20),
    )(*(pltpu.with_memory_space_constraint(operand, pltpu.HBM) for operand in operands))


def solution(mesh):
    NZ = 16
    NY = mesh.shape["seq"] // NZ
    NH = mesh.shape["head"]
    in_specs = (
        P("seq", "head"), P(), P("seq", "head"), P("seq", "head"), P("seq", "head"), P("head"), P("head"),
    )
    return jax.shard_map(
        functools.partial(shards, NH, NY, NZ), mesh=mesh, in_specs=in_specs, out_specs=P("seq", "head"), check_vma=False)
```

```python
import functools
import math

import jax
import jax.numpy as jnp
from jax import lax
from jax.experimental import pallas as pl
from jax.experimental.pallas import tpu as pltpu
from jax.sharding import PartitionSpec as P

MESH = pl.DeviceIdType.MESH
F32, BF16 = jnp.float32, jnp.bfloat16
T = 256
HEADS = 16
HEAD_DIM = 64
STATE = 128
COLS = HEADS * HEAD_DIM
CHUNKS = 2
CHUNK = COLS // CHUNKS
CW = CHUNK // 2
LOG2E = math.log2(math.e)


def dot(a, b):
    return jnp.dot(a, b, preferred_element_type=F32)


def kernel(
    NH, NY, NZ,
    hid, w, x, g, dt, rate, gain, out,
    hid_v, w_v, x_v, g_v, dt_v, rate_v, gain_v, in_sem,
    part, rsr, agr, scl, wgt, expand,
    fsend, frecv, dsend, drecv, ysend, yrecv, gsend, grecv,
    acc, fac, gated_v, srecv,
    rs_s, rs_r, ag_s, ag_r, d_s, d_r, f_s, f_r, y_s, y_r, g_s, g_r, s_s, s_r, token,
):
    KD = hid_v.shape[1]
    RB = T // NH
    NI = NZ // 2
    SR = STATE // NI
    me_h = lax.axis_index("head")
    seq = lax.axis_index("seq")
    me_z = lax.rem(seq, NZ)
    me_y = lax.div(seq, NZ)

    def head_peer(r):
        return lax.rem(me_h + r, NH)

    def far_first(k):
        off = lax.div(k, 2)
        return NZ // 2 + jnp.where(lax.rem(k, 2) == 1, off, -off)

    def z_peer(k):
        return lax.rem(me_z + far_first(k), NZ)

    def y_peer(r):
        return lax.rem(me_y + r, NY)

    def seq_id(y, z):
        return y * NZ + z

    def each(n, peer_of, action):
        @pl.loop(1, n)
        def _(r):
            action(peer_of(r))

    def signal(sem, device):
        pl.semaphore_signal(sem, inc=1, device_id=device, device_id_type=MESH)

    barrier = pltpu.get_barrier_semaphore()
    def greet(sem, distance):
        for step in (distance, NZ - distance):
            signal(sem, {"seq": seq_id(me_y, lax.rem(me_z + step, NZ))})

    greet(barrier, 1)
    greet(barrier, 2)
    strides = []
    while 2 * 2 ** len(strides) < NZ // 2:
        strides.append(2 * 2 ** len(strides))
    each(NY, y_peer, lambda p: signal(barrier, {"seq": seq_id(p, me_z)}))
    each(NH, head_peer, lambda p: signal(barrier, {"head": p}))

    loads = [
        pltpu.make_async_copy(hid, hid_v, in_sem.at[0]),
        pltpu.make_async_copy(w.at[pl.ds(pl.multiple_of(me_h * KD, KD), KD)], w_v, in_sem.at[1]),
        pltpu.make_async_copy(dt, dt_v, in_sem.at[2]),
        pltpu.make_async_copy(rate, rate_v, in_sem.at[3]),
        pltpu.make_async_copy(x, x_v, in_sem.at[4]),
        pltpu.make_async_copy(g, g_v, in_sem.at[5]),
        pltpu.make_async_copy(gain, gain_v, in_sem.at[6]),
    ]
    for load in loads:
        load.start()
    loads[0].wait()
    loads[1].wait()
    own = dot(hid_v[...], w_v[...])
    for m in range(2):
        part[m] = own[:, STATE * m:STATE * m + STATE].reshape(NH, RB, STATE)

    def remote(src, dst, send_sem, recv_sem, device):
        return pltpu.make_async_remote_copy(
            src_ref=src, dst_ref=dst, send_sem=send_sem, recv_sem=recv_sem, device_id=device, device_id_type=MESH)

    def drain(ref, sem):
        pltpu.make_async_copy(ref, ref, sem).wait()

    def rs_copy(m, peer, slot):
        return remote(part.at[m, peer], rsr.at[m, slot], rs_s, rs_r.at[m], {"head": peer})

    def ag_copy(m, peer, slot):
        return remote(agr.at[m, slot], agr.at[m, slot], ag_s, ag_r.at[m], {"head": peer})

    def d_copy(peer, slot):
        return remote(dsend.at[lax.div(peer, NI)], drecv.at[slot], d_s, d_r, {"seq": seq_id(me_y, peer)})

    def f_copy(c, peer, slot):
        return remote(fsend.at[c, peer], frecv.at[c, slot], f_s, f_r.at[c], {"seq": seq_id(me_y, peer)})

    def y_copy(c, peer, slot):
        return remote(ysend.at[c], yrecv.at[c, slot], y_s, y_r.at[c], {"seq": seq_id(peer, me_z)})

    def g_copy(c, peer, slot):
        return remote(gsend.at[c, peer], grecv.at[c, slot], g_s, g_r.at[c], {"seq": seq_id(me_y, peer)})

    def s_copy(peer, slot):
        return remote(srecv.at[slot], srecv.at[slot], s_s, s_r, {"head": peer})

    pl.semaphore_wait(barrier, (NH - 1) + (NY - 1) + 4)
    greet(token.at[0], strides[0])
    for m in range(2):
        each(NH, head_peer, lambda p: rs_copy(m, p, me_h).start())

    loads[2].wait()
    loads[3].wait()
    lane = lax.broadcasted_iota(jnp.int32, (T, 128), 1)
    low_lane = lane < HEAD_DIM
    rows = lax.broadcasted_iota(jnp.int32, (T, T), 0)
    cols = lax.broadcasted_iota(jnp.int32, (T, T), 1)
    causal = rows >= cols
    tri = jnp.where(causal, 1.0, 0.0).astype(BF16)
    dt_all = jnp.concatenate([dt_v[...], jnp.zeros((128 - HEADS, T), F32)], axis=0).T
    rate_all = jnp.concatenate([rate_v[...], jnp.zeros((1, 128 - HEADS), F32)], axis=1)
    log_decay = -(dt_all * rate_all)
    top = log_decay.astype(BF16)
    rest = log_decay - top.astype(F32)
    mid = rest.astype(BF16)
    low = (rest - mid.astype(F32)).astype(BF16)
    cum = ((dot(tri, low) + dot(tri, mid)) + dot(tri, top)) * LOG2E
    cum_end = cum[T - 1:T, :]
    grow = jnp.exp2(cum)
    tail = jnp.exp2(cum_end - cum)

    def spread(value, q):
        a = jnp.broadcast_to(value[:, 2 * q:2 * q + 1], (T, 128))
        b = jnp.broadcast_to(value[:, 2 * q + 1:2 * q + 2], (T, 128))
        return jnp.where(low_lane, a, b)

    for q in range(HEADS // 2):
        at = pl.ds(128 * q, 128)
        e = spread(grow, q)
        expand[:, at] = e
        dsend[(q % 4) // 2, q // 4, :, pl.ds(128 * (q % 2), 128)] = e[T - 1:T, :]
    for i, stride in enumerate(strides[1:]):
        pl.semaphore_wait(token.at[i], 2)
        greet(token.at[i + 1], stride)

    loads[4].wait()
    for q in range(HEADS // 2):
        at = pl.ds(128 * q, 128)
        s = (x_v[:, at].astype(F32) * spread(dt_all, q)).astype(BF16)
        scl[:, at] = s
        wgt[:, at] = (spread(tail, q) * s.astype(F32)).astype(BF16)

    for m in range(2):
        rsr[m, pl.ds(me_h, 1)] = part[m, pl.ds(me_h, 1)]
        drain(rsr.at[m, pl.ds(0, NH - 1)], rs_r.at[m])
        total = rsr[m, 0]
        for k in range(1, NH):
            total = total + rsr[m, k]
        agr[m, pl.ds(me_h, 1)] = total.astype(BF16)[None]
        each(NH, head_peer, lambda p: ag_copy(m, p, me_h).start())
    pl.semaphore_wait(token.at[len(strides) - 1], 2)
    each(NZ, z_peer, lambda p: d_copy(p, me_z).start())
    drecv[pl.ds(me_z, 1)] = dsend[pl.ds(lax.div(me_z, NI), 1)]
    drain(agr.at[0, pl.ds(0, NH - 1)], ag_r.at[0])
    b_cols = agr[0].reshape(T, STATE).astype(F32).T.astype(BF16)


    for c in range(CHUNKS):
        fresh = dot(b_cols, wgt[:, pl.ds(CHUNK * c, CHUNK)]).astype(BF16)
        for j in range(2):
            fsend[c, pl.ds(NI * j, NI)] = fresh[:, CW * j:CW * j + CW].reshape(NI, SR, CW)
        each(NZ, z_peer, lambda p: f_copy(c, p, me_z).start())
        frecv[c, pl.ds(me_z, 1)] = fsend[c, pl.ds(me_z, 1)]

    drain(agr.at[1, pl.ds(0, NH - 1)], ag_r.at[1])
    c_rows = agr[1].reshape(T, STATE)
    loads[5].wait()
    scores = dot(c_rows, b_cols)
    M = T // 2
    tri_half = causal[:M, :M]
    s00 = jnp.where(tri_half, scores[:M, :M], 0.0)
    s10 = scores[M:, :M]
    s11 = jnp.where(tri_half, scores[M:, M:], 0.0)
    cum_rows = cum.T
    for q in range(HEADS // 2):
        at = pl.ds(128 * q, 128)
        mix = []
        for h in (2 * q, 2 * q + 1):
            down = jnp.broadcast_to(cum[:, h:h + 1], (T, M))
            along = cum_rows[h:h + 1, :]
            m00 = s00 * jnp.exp2(jnp.minimum(down[:M] - along[:, :M], 0.0))
            m10 = s10 * jnp.exp2(down[M:] - along[:, :M])
            m11 = s11 * jnp.exp2(jnp.minimum(down[M:] - along[:, M:], 0.0))
            mix.append((m00.astype(BF16), jnp.concatenate([m10.astype(BF16), m11.astype(BF16)], axis=1)))
        s = scl[:, at]
        zero = jnp.zeros_like(s)
        sa = jnp.where(low_lane, s, zero)
        sb = jnp.where(low_lane, zero, s)
        upper = dot(jnp.concatenate([mix[0][0], mix[1][0]], axis=1), jnp.concatenate([sa[:M], sb[:M]], axis=0))
        lower = dot(mix[0][1], sa) + dot(mix[1][1], sb)
        v = g_v[:, at].astype(F32)
        silu = v / (1.0 + jnp.exp(-v))
        fac[:, at] = expand[:, at] * silu
        acc[:M, at] = upper * silu[:M]
        acc[M:, at] = lower * silu[M:]

    drain(drecv.at[pl.ds(0, NZ - 1)], d_r)
    for c in range(CHUNKS):
        drain(frecv.at[c, pl.ds(0, NZ - 1)], f_r.at[c])
        carry = frecv[c, 0].astype(F32)
        span = drecv[0, c]
        for k in range(1, NZ):
            carry = drecv[k, c] * carry + frecv[c, k].astype(F32)
            span = drecv[k, c] * span
        ysend[c, :SR] = carry
        ysend[c, SR:] = jnp.broadcast_to(span, (8, CW))
        each(NY, y_peer, lambda p: y_copy(c, p, me_y).start())
        yrecv[c, pl.ds(me_y, 1)] = ysend[c][None]
    for c in range(CHUNKS):
        if NY > 1:
            drain(yrecv.at[c, pl.ds(0, NY - 1)], y_r.at[c])
        carry = jnp.zeros((SR, CW), F32)
        for k in range(NY - 1):
            later = yrecv[c, k, SR:SR + 1] * carry + yrecv[c, k, :SR]
            carry = jnp.where(k < me_y, later, carry)
        for k in range(NZ):
            gsend[c, k] = carry.astype(BF16)
            carry = drecv[k, c] * carry + frecv[c, k].astype(F32)
        each(NZ, z_peer, lambda p: g_copy(c, p, me_z).start())
        grecv[c, pl.ds(me_z, 1)] = gsend[c, pl.ds(me_z, 1)]

    loads[6].wait()
    squares = jnp.zeros((T, 128), F32)
    for c in range(CHUNKS):
        drain(grecv.at[c, pl.ds(0, NZ - 1)], g_r.at[c])
        for j in range(2):
            entering = grecv[c, pl.ds(NI * j, NI)].reshape(STATE, CW)
            at = pl.ds(CHUNK * c + CW * j, CW)
            gated = acc[:, at] + dot(c_rows, entering) * fac[:, at]
            gated_v[:, at] = gated * gain_v[:, at]
            sq = gated * gated
            for i in range(CW // 128):
                squares = squares + sq[:, 128 * i:128 * i + 128]
    srecv[pl.ds(me_h, 1)] = jnp.sum(squares.T, axis=0, keepdims=True)[None]
    each(NH, head_peer, lambda p: s_copy(p, me_h).start())
    drain(srecv.at[pl.ds(0, NH - 1)], s_r)
    mean = srecv[0]
    for k in range(1, NH):
        mean = mean + srecv[k]
    mean = mean / (NH * COLS)
    scale = lax.rsqrt(jnp.broadcast_to(mean, (128, T)) + 1e-05).T
    for q in range(HEADS // 2):
        at = pl.ds(128 * q, 128)
        out[:, at] = (gated_v[:, at] * scale).astype(BF16)

    drain(part.at[:, pl.ds(0, NH - 1)], rs_s)
    drain(agr.at[:, pl.ds(0, NH - 1)], ag_s)
    drain(drecv.at[pl.ds(0, NZ - 1)], d_s)
    drain(fsend.at[:, pl.ds(0, NZ - 1)], f_s)
    drain(gsend.at[:, pl.ds(0, NZ - 1)], g_s)
    drain(srecv.at[pl.ds(0, NH - 1)], s_s)
    if NY > 1:
        drain(yrecv.at[:, pl.ds(0, NY - 1)], y_s)


def shards(NH, NY, NZ, hidden_in, proj_weight, head_input, gate_input, step_size, decay_rate, norm_gain):
    KD = hidden_in.shape[1]
    RB = T // NH
    SR = STATE // (NZ // 2)
    operands = (hidden_in, proj_weight, head_input, gate_input, step_size.T, decay_rate.reshape(1, HEADS), norm_gain.reshape(1, COLS))
    in_hbm = pl.BlockSpec(memory_space=pltpu.HBM)
    vm, dma = pltpu.VMEM, pltpu.SemaphoreType.DMA
    return pl.pallas_call(
        functools.partial(kernel, NH, NY, NZ),
        name="layer",
        out_shape=jax.ShapeDtypeStruct((T, COLS), BF16),
        in_specs=[in_hbm] * 7,
        out_specs=pl.BlockSpec(memory_space=pltpu.VMEM),
        scratch_shapes=[
            vm((T, KD), BF16), vm((KD, 2 * STATE), BF16), vm((T, COLS), BF16), vm((T, COLS), BF16),
            vm((HEADS, T), F32), vm((1, HEADS), F32), vm((1, COLS), F32), dma((7,)),
            vm((2, NH, RB, STATE), F32), vm((2, NH, RB, STATE), F32), vm((2, NH, RB, STATE), BF16),
            vm((T, COLS), BF16), vm((T, COLS), BF16), vm((T, COLS), F32),
            vm((CHUNKS, NZ, SR, CW), BF16), vm((CHUNKS, NZ, SR, CW), BF16), vm((2, CHUNKS, 1, CW), F32), vm((NZ, CHUNKS, 1, CW), F32),
            vm((CHUNKS, SR + 8, CW), F32), vm((CHUNKS, NY, SR + 8, CW), F32),
            vm((CHUNKS, NZ, SR, CW), BF16), vm((CHUNKS, NZ, SR, CW), BF16),
            vm((T, COLS), F32), vm((T, COLS), F32), vm((T, COLS), F32), vm((NH, 1, T), F32),
            dma, dma((2,)), dma, dma((2,)), dma, dma, dma, dma((CHUNKS,)), dma, dma((CHUNKS,)), dma, dma((CHUNKS,)), dma, dma,
            pltpu.SemaphoreType.REGULAR((2,)),
        ],
        compiler_params=pltpu.CompilerParams(collective_id=0, has_side_effects=True, vmem_limit_bytes=20 * 2**20),
    )(*(pltpu.with_memory_space_constraint(operand, pltpu.HBM) for operand in operands))


def solution(mesh):
    NZ = 16
    NY = mesh.shape["seq"] // NZ
    NH = mesh.shape["head"]
    in_specs = (
        P("seq", "head"), P(), P("seq", "head"), P("seq", "head"), P("seq", "head"), P("head"), P("head"),
    )
    return jax.shard_map(
        functools.partial(shards, NH, NY, NZ), mesh=mesh, in_specs=in_specs, out_specs=P("seq", "head"), check_vma=False)
```

```python
import functools
import math

import jax
import jax.numpy as jnp
from jax import lax
from jax.experimental import pallas as pl
from jax.experimental.pallas import tpu as pltpu
from jax.sharding import PartitionSpec as P

MESH = pl.DeviceIdType.MESH
F32, BF16 = jnp.float32, jnp.bfloat16
T = 256
HEADS = 16
HEAD_DIM = 64
STATE = 128
COLS = HEADS * HEAD_DIM
CHUNKS = 2
CHUNK = COLS // CHUNKS
CW = CHUNK // 2
LOG2E = math.log2(math.e)


def dot(a, b):
    return jnp.dot(a, b, preferred_element_type=F32)


def kernel(
    NH, NY, NZ,
    hid, w, x, g, dt, rate, gain, out,
    hid_v, w_v, x_v, g_v, dt_v, rate_v, gain_v, in_sem,
    part, pair, agr, scl, wgt, expand,
    fsend, frecv, dsend, drecv, ysend, yrecv, gsend, grecv,
    acc, fac, gated_v, srecv,
    p_s, p_r, ag_s, ag_r, d_s, d_r, f_s, f_r, y_s, y_r, g_s, g_r, s_s, s_r, token,
):
    KD = hid_v.shape[1]
    NI = NZ // 2
    SR = STATE // NI
    me_h = lax.axis_index("head")
    core = lax.rem(me_h, 2)
    seq = lax.axis_index("seq")
    me_z = lax.rem(seq, NZ)
    me_y = lax.div(seq, NZ)

    def head_peer(r):
        return lax.rem(me_h + r, NH)

    def far_first(k):
        off = lax.div(k, 2)
        return NZ // 2 + jnp.where(lax.rem(k, 2) == 1, off, -off)

    def z_peer(k):
        return lax.rem(me_z + far_first(k), NZ)

    def y_peer(r):
        return lax.rem(me_y + r, NY)

    def seq_id(y, z):
        return y * NZ + z

    def each(n, peer_of, action):
        @pl.loop(1, n)
        def _(r):
            action(peer_of(r))

    def each_now(n, peer_of, action):
        for r in range(1, n):
            action(peer_of(r))

    def signal(sem, device):
        pl.semaphore_signal(sem, inc=1, device_id=device, device_id_type=MESH)

    loads = [
        pltpu.make_async_copy(hid, hid_v, in_sem.at[0]),
        pltpu.make_async_copy(w.at[pl.ds(pl.multiple_of(me_h * KD, KD), KD)], w_v, in_sem.at[1]),
        pltpu.make_async_copy(dt, dt_v, in_sem.at[2]),
        pltpu.make_async_copy(rate, rate_v, in_sem.at[3]),
        pltpu.make_async_copy(x, x_v, in_sem.at[4]),
        pltpu.make_async_copy(g, g_v, in_sem.at[5]),
        pltpu.make_async_copy(gain, gain_v, in_sem.at[6]),
    ]
    loads[0].start()
    loads[1].start()

    barrier = pltpu.get_barrier_semaphore()
    def greet(sem, distance):
        for step in (distance, NZ - distance):
            signal(sem, {"seq": seq_id(me_y, lax.rem(me_z + step, NZ))})

    greet(barrier, 1)
    greet(barrier, 2)
    strides = []
    while 2 * 2 ** len(strides) < NZ // 2:
        strides.append(2 * 2 ** len(strides))
    each_now(NY, y_peer, lambda p: signal(barrier, {"seq": seq_id(p, me_z)}))
    each_now(NH, head_peer, lambda p: signal(barrier, {"head": p}))

    for load in loads[2:]:
        load.start()
    loads[0].wait()
    loads[1].wait()
    own = dot(hid_v[...], w_v[...])
    for m in range(2):
        part[m] = own[:, STATE * m:STATE * m + STATE].reshape(2, T // 2, STATE)

    def remote(src, dst, send_sem, recv_sem, device):
        return pltpu.make_async_remote_copy(
            src_ref=src, dst_ref=dst, send_sem=send_sem, recv_sem=recv_sem, device_id=device, device_id_type=MESH)

    def drain(ref, sem):
        pltpu.make_async_copy(ref, ref, sem).wait()

    def pair_copy(m):
        return remote(part.at[m, 1 - core], pair.at[m], p_s, p_r.at[m], {"head": me_h + 1 - 2 * core})

    def ag_copy(m, peer, slot):
        return remote(agr.at[m, slot], agr.at[m, slot], ag_s, ag_r.at[m], {"head": peer})

    def d_copy(peer, slot):
        return remote(dsend.at[lax.div(peer, NI)], drecv.at[slot], d_s, d_r, {"seq": seq_id(me_y, peer)})

    def f_copy(c, peer, slot):
        return remote(fsend.at[c, peer], frecv.at[c, slot], f_s, f_r.at[c], {"seq": seq_id(me_y, peer)})

    def y_copy(c, peer, slot):
        return remote(ysend.at[c], yrecv.at[c, slot], y_s, y_r.at[c], {"seq": seq_id(peer, me_z)})

    def g_copy(c, peer, slot):
        return remote(gsend.at[c, peer], grecv.at[c, slot], g_s, g_r.at[c], {"seq": seq_id(me_y, peer)})

    def s_copy(peer, slot):
        return remote(srecv.at[slot], srecv.at[slot], s_s, s_r, {"head": peer})

    pl.semaphore_wait(barrier, (NH - 1) + (NY - 1) + 4)
    greet(token.at[0], strides[0])
    for m in range(2):
        pair_copy(m).start()

    def spread_chip_sum(m):
        drain(pair.at[m], p_r.at[m])
        agr[m, pl.ds(me_h, 1)] = (part[m, pl.ds(core, 1)] + pair[m][None]).astype(BF16)
        each_now(NH, head_peer, lambda p: ag_copy(m, p, me_h).start())

    spread_chip_sum(0)

    def projected(m):
        drain(agr.at[m, pl.ds(0, NH - 1)], ag_r.at[m])
        halves = []
        for i in range(2):
            total = agr[m, i].astype(F32)
            for k in range(2 + i, NH, 2):
                total = total + agr[m, k].astype(F32)
            halves.append(total)
        return jnp.concatenate(halves, axis=0).astype(BF16)

    loads[2].wait()
    loads[3].wait()
    lane = lax.broadcasted_iota(jnp.int32, (T, 128), 1)
    low_lane = lane < HEAD_DIM
    rows = lax.broadcasted_iota(jnp.int32, (T, T), 0)
    cols = lax.broadcasted_iota(jnp.int32, (T, T), 1)
    causal = rows >= cols
    tri = jnp.where(causal, 1.0, 0.0).astype(BF16)
    dt_all = jnp.concatenate([dt_v[...], jnp.zeros((128 - HEADS, T), F32)], axis=0).T
    rate_all = jnp.concatenate([rate_v[...], jnp.zeros((1, 128 - HEADS), F32)], axis=1)
    log_decay = -(dt_all * rate_all)
    top = log_decay.astype(BF16)
    rest = log_decay - top.astype(F32)
    mid = rest.astype(BF16)
    low = (rest - mid.astype(F32)).astype(BF16)
    cum = ((dot(tri, low) + dot(tri, mid)) + dot(tri, top)) * LOG2E
    cum_end = cum[T - 1:T, :]
    grow = jnp.exp2(cum)
    tail = jnp.exp2(cum_end - cum)

    def spread(value, q):
        a = jnp.broadcast_to(value[:, 2 * q:2 * q + 1], (T, 128))
        b = jnp.broadcast_to(value[:, 2 * q + 1:2 * q + 2], (T, 128))
        return jnp.where(low_lane, a, b)

    for q in range(HEADS // 2):
        at = pl.ds(128 * q, 128)
        e = spread(grow, q)
        expand[:, at] = e
        dsend[(q % 4) // 2, q // 4, :, pl.ds(128 * (q % 2), 128)] = e[T - 1:T, :]
    for i, stride in enumerate(strides[1:]):
        pl.semaphore_wait(token.at[i], 2)
        greet(token.at[i + 1], stride)

    spread_chip_sum(1)
    loads[4].wait()
    for q in range(HEADS // 2):
        at = pl.ds(128 * q, 128)
        s = (x_v[:, at].astype(F32) * spread(dt_all, q)).astype(BF16)
        scl[:, at] = s
        wgt[:, at] = (spread(tail, q) * s.astype(F32)).astype(BF16)

    pl.semaphore_wait(token.at[len(strides) - 1], 2)
    each(NZ, z_peer, lambda p: d_copy(p, me_z).start())
    drecv[pl.ds(me_z, 1)] = dsend[pl.ds(lax.div(me_z, NI), 1)]
    b_cols = projected(0).astype(F32).T.astype(BF16)


    for c in range(CHUNKS):
        fresh = dot(b_cols, wgt[:, pl.ds(CHUNK * c, CHUNK)]).astype(BF16)
        for j in range(2):
            fsend[c, pl.ds(NI * j, NI)] = fresh[:, CW * j:CW * j + CW].reshape(NI, SR, CW)
        each(NZ, z_peer, lambda p: f_copy(c, p, me_z).start())
        frecv[c, pl.ds(me_z, 1)] = fsend[c, pl.ds(me_z, 1)]

    c_rows = projected(1)
    loads[5].wait()
    scores = dot(c_rows, b_cols)
    M = T // 2
    tri_half = causal[:M, :M]
    s00 = jnp.where(tri_half, scores[:M, :M], 0.0)
    s10 = scores[M:, :M]
    s11 = jnp.where(tri_half, scores[M:, M:], 0.0)
    cum_rows = cum.T
    for q in range(HEADS // 2):
        at = pl.ds(128 * q, 128)
        mix = []
        for h in (2 * q, 2 * q + 1):
            down = jnp.broadcast_to(cum[:, h:h + 1], (T, M))
            along = cum_rows[h:h + 1, :]
            m00 = s00 * jnp.exp2(jnp.minimum(down[:M] - along[:, :M], 0.0))
            m10 = s10 * jnp.exp2(down[M:] - along[:, :M])
            m11 = s11 * jnp.exp2(jnp.minimum(down[M:] - along[:, M:], 0.0))
            mix.append((m00.astype(BF16), jnp.concatenate([m10.astype(BF16), m11.astype(BF16)], axis=1)))
        s = scl[:, at]
        zero = jnp.zeros_like(s)
        sa = jnp.where(low_lane, s, zero)
        sb = jnp.where(low_lane, zero, s)
        upper = dot(jnp.concatenate([mix[0][0], mix[1][0]], axis=1), jnp.concatenate([sa[:M], sb[:M]], axis=0))
        lower = dot(mix[0][1], sa) + dot(mix[1][1], sb)
        v = g_v[:, at].astype(F32)
        silu = v / (1.0 + jnp.exp(-v))
        fac[:, at] = expand[:, at] * silu
        acc[:M, at] = upper * silu[:M]
        acc[M:, at] = lower * silu[M:]

    drain(drecv.at[pl.ds(0, NZ - 1)], d_r)
    for c in range(CHUNKS):
        drain(frecv.at[c, pl.ds(0, NZ - 1)], f_r.at[c])
        carry = frecv[c, 0].astype(F32)
        span = drecv[0, c]
        for k in range(1, NZ):
            carry = drecv[k, c] * carry + frecv[c, k].astype(F32)
            span = drecv[k, c] * span
        ysend[c, :SR] = carry
        ysend[c, SR:] = jnp.broadcast_to(span, (8, CW))
        each_now(NY, y_peer, lambda p: y_copy(c, p, me_y).start())
        yrecv[c, pl.ds(me_y, 1)] = ysend[c][None]
    for c in range(CHUNKS):
        if NY > 1:
            drain(yrecv.at[c, pl.ds(0, NY - 1)], y_r.at[c])
        carry = jnp.zeros((SR, CW), F32)
        for k in range(NY - 1):
            later = yrecv[c, k, SR:SR + 1] * carry + yrecv[c, k, :SR]
            carry = jnp.where(k < me_y, later, carry)
        for k in range(NZ):
            gsend[c, k] = carry.astype(BF16)
            carry = drecv[k, c] * carry + frecv[c, k].astype(F32)
        each(NZ, z_peer, lambda p: g_copy(c, p, me_z).start())
        grecv[c, pl.ds(me_z, 1)] = gsend[c, pl.ds(me_z, 1)]

    loads[6].wait()
    squares = jnp.zeros((T, 128), F32)
    for c in range(CHUNKS):
        drain(grecv.at[c, pl.ds(0, NZ - 1)], g_r.at[c])
        for j in range(2):
            entering = grecv[c, pl.ds(NI * j, NI)].reshape(STATE, CW)
            at = pl.ds(CHUNK * c + CW * j, CW)
            gated = acc[:, at] + dot(c_rows, entering) * fac[:, at]
            gated_v[:, at] = gated * gain_v[:, at]
            sq = gated * gated
            for i in range(CW // 128):
                squares = squares + sq[:, 128 * i:128 * i + 128]
    srecv[pl.ds(me_h, 1)] = jnp.sum(squares.T, axis=0, keepdims=True)[None]
    each_now(NH, head_peer, lambda p: s_copy(p, me_h).start())
    drain(srecv.at[pl.ds(0, NH - 1)], s_r)
    mean = srecv[0]
    for k in range(1, NH):
        mean = mean + srecv[k]
    mean = mean / (NH * COLS)
    scale = lax.rsqrt(jnp.broadcast_to(mean, (128, T)) + 1e-05).T
    for q in range(HEADS // 2):
        at = pl.ds(128 * q, 128)
        out[:, at] = (gated_v[:, at] * scale).astype(BF16)

    drain(pair, p_s)
    drain(agr.at[:, pl.ds(0, NH - 1)], ag_s)
    drain(drecv.at[pl.ds(0, NZ - 1)], d_s)
    drain(fsend.at[:, pl.ds(0, NZ - 1)], f_s)
    drain(gsend.at[:, pl.ds(0, NZ - 1)], g_s)
    drain(srecv.at[pl.ds(0, NH - 1)], s_s)
    if NY > 1:
        drain(yrecv.at[:, pl.ds(0, NY - 1)], y_s)


def shards(NH, NY, NZ, hidden_in, proj_weight, head_input, gate_input, step_size, decay_rate, norm_gain):
    KD = hidden_in.shape[1]
    SR = STATE // (NZ // 2)
    operands = (hidden_in, proj_weight, head_input, gate_input, step_size.T, decay_rate.reshape(1, HEADS), norm_gain.reshape(1, COLS))
    in_hbm = pl.BlockSpec(memory_space=pltpu.HBM)
    vm, dma = pltpu.VMEM, pltpu.SemaphoreType.DMA
    return pl.pallas_call(
        functools.partial(kernel, NH, NY, NZ),
        name="layer",
        out_shape=jax.ShapeDtypeStruct((T, COLS), BF16),
        in_specs=[in_hbm] * 7,
        out_specs=pl.BlockSpec(memory_space=pltpu.VMEM),
        scratch_shapes=[
            vm((T, KD), BF16), vm((KD, 2 * STATE), BF16), vm((T, COLS), BF16), vm((T, COLS), BF16),
            vm((HEADS, T), F32), vm((1, HEADS), F32), vm((1, COLS), F32), dma((7,)),
            vm((2, 2, T // 2, STATE), F32), vm((2, T // 2, STATE), F32), vm((2, NH, T // 2, STATE), BF16),
            vm((T, COLS), BF16), vm((T, COLS), BF16), vm((T, COLS), F32),
            vm((CHUNKS, NZ, SR, CW), BF16), vm((CHUNKS, NZ, SR, CW), BF16), vm((2, CHUNKS, 1, CW), F32), vm((NZ, CHUNKS, 1, CW), F32),
            vm((CHUNKS, SR + 8, CW), F32), vm((CHUNKS, NY, SR + 8, CW), F32),
            vm((CHUNKS, NZ, SR, CW), BF16), vm((CHUNKS, NZ, SR, CW), BF16),
            vm((T, COLS), F32), vm((T, COLS), F32), vm((T, COLS), F32), vm((NH, 1, T), F32),
            dma, dma((2,)), dma, dma((2,)), dma, dma, dma, dma((CHUNKS,)), dma, dma((CHUNKS,)), dma, dma((CHUNKS,)), dma, dma,
            pltpu.SemaphoreType.REGULAR((2,)),
        ],
        compiler_params=pltpu.CompilerParams(collective_id=0, has_side_effects=True, vmem_limit_bytes=20 * 2**20),
    )(*(pltpu.with_memory_space_constraint(operand, pltpu.HBM) for operand in operands))


def solution(mesh):
    NZ = 16
    NY = mesh.shape["seq"] // NZ
    NH = mesh.shape["head"]
    in_specs = (
        P("seq", "head"), P(), P("seq", "head"), P("seq", "head"), P("seq", "head"), P("head"), P("head"),
    )
    return jax.shard_map(
        functools.partial(shards, NH, NY, NZ), mesh=mesh, in_specs=in_specs, out_specs=P("seq", "head"), check_vma=False)
```

```python
import functools
import math

import jax
import jax.numpy as jnp
from jax import lax
from jax.experimental import pallas as pl
from jax.experimental.pallas import tpu as pltpu
from jax.sharding import PartitionSpec as P

MESH = pl.DeviceIdType.MESH
F32, BF16 = jnp.float32, jnp.bfloat16
T = 256
HEADS = 16
HEAD_DIM = 64
STATE = 128
COLS = HEADS * HEAD_DIM
LAG = 1
CHUNKS = 4
CHUNK = COLS // CHUNKS
CW = CHUNK // 2
LOG2E = math.log2(math.e)


def dot(a, b):
    return jnp.dot(a, b, preferred_element_type=F32)


def kernel(
    NH, NY, NZ,
    hid, w, x, g, dt, rate, gain, out,
    hid_v, w_v, x_v, g_v, dt_v, rate_v, gain_v, in_sem,
    part, pair, agr, scl, wgt, expand,
    fsend, frecv, dsend, drecv, zsend, zrecv, ysend, yrecv, gsend, grecv,
    acc, fac, gated_v, srecv,
    p_s, p_r, ag_s, ag_r, d_s, d_r, f_s, f_r, z_s, z_r, y_s, y_r, g_s, g_r, s_s, s_r, token,
):
    KD = hid_v.shape[1]
    NI = NZ // 2
    SR = STATE // NI
    me_h = lax.axis_index("head")
    core = lax.rem(me_h, 2)
    seq = lax.axis_index("seq")
    me_z = lax.rem(seq, NZ)
    me_y = lax.div(seq, NZ)

    def head_peer(r):
        return lax.rem(me_h + r, NH)

    def far_first(k):
        return NZ // 2 + (k // 2 if k % 2 else -(k // 2))

    def z_peer(k):
        return lax.rem(me_z + far_first(k), NZ)

    def y_peer(r):
        return lax.rem(me_y + r, NY)

    def seq_id(y, z):
        return y * NZ + z

    def each_now(n, peer_of, action):
        for r in range(1, n):
            action(peer_of(r))

    def signal(sem, device):
        pl.semaphore_signal(sem, inc=1, device_id=device, device_id_type=MESH)

    loads = [
        pltpu.make_async_copy(hid, hid_v, in_sem.at[0]),
        pltpu.make_async_copy(w.at[pl.ds(pl.multiple_of(me_h * KD, KD), KD)], w_v, in_sem.at[1]),
        pltpu.make_async_copy(dt, dt_v, in_sem.at[2]),
        pltpu.make_async_copy(rate, rate_v, in_sem.at[3]),
        pltpu.make_async_copy(x, x_v, in_sem.at[4]),
        pltpu.make_async_copy(g, g_v, in_sem.at[5]),
        pltpu.make_async_copy(gain, gain_v, in_sem.at[6]),
    ]
    loads[0].start()
    loads[1].start()

    barrier = pltpu.get_barrier_semaphore()
    def greet(sem, distance):
        for step in (distance, NZ - distance):
            signal(sem, {"seq": seq_id(me_y, lax.rem(me_z + step, NZ))})

    greet(barrier, 1)
    greet(barrier, 2)
    strides = []
    while 2 * 2 ** len(strides) < NZ // 2:
        strides.append(2 * 2 ** len(strides))
    each_now(NY, y_peer, lambda p: signal(barrier, {"seq": seq_id(p, me_z)}))
    each_now(NH, head_peer, lambda p: signal(barrier, {"head": p}))

    for load in loads[2:]:
        load.start()
    loads[0].wait()
    loads[1].wait()
    own = dot(hid_v[...], w_v[...])
    for m in range(2):
        part[m] = own[:, STATE * m:STATE * m + STATE].reshape(2, T // 2, STATE)

    def remote(src, dst, send_sem, recv_sem, device):
        return pltpu.make_async_remote_copy(
            src_ref=src, dst_ref=dst, send_sem=send_sem, recv_sem=recv_sem, device_id=device, device_id_type=MESH)

    def drain(ref, sem):
        pltpu.make_async_copy(ref, ref, sem).wait()

    def pair_copy(m):
        return remote(part.at[m, 1 - core], pair.at[m], p_s, p_r.at[m], {"head": me_h + 1 - 2 * core})

    def ag_copy(m, peer, slot):
        return remote(agr.at[m, slot], agr.at[m, slot], ag_s, ag_r.at[m], {"head": peer})

    def d_copy(peer, slot):
        return remote(dsend.at[lax.div(peer, NI)], drecv.at[slot], d_s, d_r, {"seq": seq_id(me_y, peer)})

    def f_copy(c, peer, slot):
        return remote(fsend.at[c, peer], frecv.at[c, slot], f_s, f_r.at[c], {"seq": seq_id(me_y, peer)})

    def y_copy(c, peer, slot):
        return remote(ysend.at[c], yrecv.at[c, slot], y_s, y_r.at[c], {"seq": seq_id(peer, me_z)})

    def span_copy(peer, slot):
        return remote(zsend, zrecv.at[slot], z_s, z_r, {"seq": seq_id(peer, me_z)})

    def g_copy(c, peer, slot):
        return remote(gsend.at[c, peer], grecv.at[c, slot], g_s, g_r.at[c], {"seq": seq_id(me_y, peer)})

    def s_copy(peer, slot):
        return remote(srecv.at[slot], srecv.at[slot], s_s, s_r, {"head": peer})

    pl.semaphore_wait(barrier, (NH - 1) + (NY - 1) + 4)
    greet(token.at[0], strides[0])
    for m in range(2):
        pair_copy(m).start()

    def spread_chip_sum(m):
        drain(pair.at[m], p_r.at[m])
        agr[m, pl.ds(me_h, 1)] = (part[m, pl.ds(core, 1)] + pair[m][None]).astype(BF16)
        each_now(NH, head_peer, lambda p: ag_copy(m, p, me_h).start())

    spread_chip_sum(0)

    def projected(m):
        drain(agr.at[m, pl.ds(0, NH - 1)], ag_r.at[m])
        halves = []
        for i in range(2):
            total = agr[m, i].astype(F32)
            for k in range(2 + i, NH, 2):
                total = total + agr[m, k].astype(F32)
            halves.append(total)
        return jnp.concatenate(halves, axis=0).astype(BF16)

    loads[2].wait()
    loads[3].wait()
    lane = lax.broadcasted_iota(jnp.int32, (T, 128), 1)
    low_lane = lane < HEAD_DIM
    rows = lax.broadcasted_iota(jnp.int32, (T, T), 0)
    cols = lax.broadcasted_iota(jnp.int32, (T, T), 1)
    causal = rows >= cols
    tri = jnp.where(causal, 1.0, 0.0).astype(BF16)
    dt_all = jnp.concatenate([dt_v[...], jnp.zeros((128 - HEADS, T), F32)], axis=0).T
    rate_all = jnp.concatenate([rate_v[...], jnp.zeros((1, 128 - HEADS), F32)], axis=1)
    log_decay = -(dt_all * rate_all)
    top = log_decay.astype(BF16)
    rest = log_decay - top.astype(F32)
    mid = rest.astype(BF16)
    low = (rest - mid.astype(F32)).astype(BF16)
    cum = ((dot(tri, low) + dot(tri, mid)) + dot(tri, top)) * LOG2E
    cum_end = cum[T - 1:T, :]
    grow = jnp.exp2(cum)
    tail = jnp.exp2(cum_end - cum)

    def spread(value, q):
        a = jnp.broadcast_to(value[:, 2 * q:2 * q + 1], (T, 128))
        b = jnp.broadcast_to(value[:, 2 * q + 1:2 * q + 2], (T, 128))
        return jnp.where(low_lane, a, b)

    for q in range(HEADS // 2):
        at = pl.ds(128 * q, 128)
        e = spread(grow, q)
        expand[:, at] = e
        dsend[q % 2, q // 2] = e[T - 1:T, :]
    for i, stride in enumerate(strides[1:]):
        pl.semaphore_wait(token.at[i], 2)
        greet(token.at[i + 1], stride)

    spread_chip_sum(1)
    loads[4].wait()
    for q in range(HEADS // 2):
        at = pl.ds(128 * q, 128)
        s = (x_v[:, at].astype(F32) * spread(dt_all, q)).astype(BF16)
        scl[:, at] = s
        wgt[:, at] = (spread(tail, q) * s.astype(F32)).astype(BF16)

    pl.semaphore_wait(token.at[len(strides) - 1], 2)
    each_now(NZ, z_peer, lambda p: d_copy(p, me_z).start())
    drecv[pl.ds(me_z, 1)] = dsend[pl.ds(lax.div(me_z, NI), 1)]
    b_cols = projected(0).astype(F32).T.astype(BF16)


    for c in range(CHUNKS):
        fresh = dot(b_cols, wgt[:, pl.ds(CHUNK * c, CHUNK)]).astype(BF16)
        for j in range(2):
            fsend[c, pl.ds(NI * j, NI)] = fresh[:, CW * j:CW * j + CW].reshape(NI, SR, CW)
        each_now(NZ, z_peer, lambda p: f_copy(c, p, me_z).start())
        frecv[c, pl.ds(me_z, 1)] = fsend[c, pl.ds(me_z, 1)]

    c_rows = projected(1)
    loads[5].wait()
    scores = dot(c_rows, b_cols)
    M = T // 2
    tri_half = causal[:M, :M]
    s00 = jnp.where(tri_half, scores[:M, :M], 0.0)
    s10 = scores[M:, :M]
    s11 = jnp.where(tri_half, scores[M:, M:], 0.0)
    cum_rows = cum.T
    for q in range(HEADS // 2):
        at = pl.ds(128 * q, 128)
        mix = []
        for h in (2 * q, 2 * q + 1):
            down = jnp.broadcast_to(cum[:, h:h + 1], (T, M))
            along = cum_rows[h:h + 1, :]
            m00 = s00 * jnp.exp2(jnp.minimum(down[:M] - along[:, :M], 0.0))
            m10 = s10 * jnp.exp2(down[M:] - along[:, :M])
            m11 = s11 * jnp.exp2(jnp.minimum(down[M:] - along[:, M:], 0.0))
            mix.append((m00.astype(BF16), jnp.concatenate([m10.astype(BF16), m11.astype(BF16)], axis=1)))
        s = scl[:, at]
        zero = jnp.zeros_like(s)
        sa = jnp.where(low_lane, s, zero)
        sb = jnp.where(low_lane, zero, s)
        upper = dot(jnp.concatenate([mix[0][0], mix[1][0]], axis=1), jnp.concatenate([sa[:M], sb[:M]], axis=0))
        lower = dot(mix[0][1], sa) + dot(mix[1][1], sb)
        v = g_v[:, at].astype(F32)
        silu = v / (1.0 + jnp.exp(-v))
        fac[:, at] = expand[:, at] * silu
        acc[:M, at] = upper * silu[:M]
        acc[M:, at] = lower * silu[M:]

    drain(drecv.at[pl.ds(0, NZ - 1)], d_r)
    span = drecv[0]
    for k in range(1, NZ):
        span = span * drecv[k]
    zsend[...] = span
    each_now(NY, y_peer, lambda p: span_copy(p, me_y).start())
    zrecv[pl.ds(me_y, 1)] = zsend[...][None]
    def total_of_row(c):
        drain(frecv.at[c, pl.ds(0, NZ - 1)], f_r.at[c])
        carry = frecv[c, 0].astype(F32)
        for k in range(1, NZ):
            carry = drecv[k, c] * carry + frecv[c, k].astype(F32)
        ysend[c] = carry
        each_now(NY, y_peer, lambda p: y_copy(c, p, me_y).start())
        yrecv[c, pl.ds(me_y, 1)] = ysend[c][None]

    def entering_states(c):
        if NY > 1:
            drain(yrecv.at[c, pl.ds(0, NY - 1)], y_r.at[c])
        carry = jnp.zeros((SR, CW), F32)
        for k in range(NY - 1):
            later = zrecv[k, c] * carry + yrecv[c, k]
            carry = jnp.where(k < me_y, later, carry)
        for k in range(NZ):
            gsend[c, k] = carry.astype(BF16)
            carry = drecv[k, c] * carry + frecv[c, k].astype(F32)
        each_now(NZ, z_peer, lambda p: g_copy(c, p, me_z).start())
        grecv[c, pl.ds(me_z, 1)] = gsend[c, pl.ds(me_z, 1)]

    for c in range(CHUNKS + LAG):
        if c < CHUNKS:
            total_of_row(c)
        if c == 0 and NY > 1:
            drain(zrecv.at[pl.ds(0, NY - 1)], z_r)
        if c >= LAG:
            entering_states(c - LAG)

    loads[6].wait()
    squares = jnp.zeros((T, 128), F32)
    for c in range(CHUNKS):
        drain(grecv.at[c, pl.ds(0, NZ - 1)], g_r.at[c])
        for j in range(2):
            entering = grecv[c, pl.ds(NI * j, NI)].reshape(STATE, CW)
            at = pl.ds(CHUNK * c + CW * j, CW)
            gated = acc[:, at] + dot(c_rows, entering) * fac[:, at]
            gated_v[:, at] = gated * gain_v[:, at]
            sq = gated * gated
            for i in range(CW // 128):
                squares = squares + sq[:, 128 * i:128 * i + 128]
    srecv[pl.ds(me_h, 1)] = jnp.sum(squares.T, axis=0, keepdims=True)[None]
    each_now(NH, head_peer, lambda p: s_copy(p, me_h).start())
    drain(srecv.at[pl.ds(0, NH - 1)], s_r)
    mean = srecv[0]
    for k in range(1, NH):
        mean = mean + srecv[k]
    mean = mean / (NH * COLS)
    scale = lax.rsqrt(jnp.broadcast_to(mean, (128, T)) + 1e-05).T
    for q in range(HEADS // 2):
        at = pl.ds(128 * q, 128)
        out[:, at] = (gated_v[:, at] * scale).astype(BF16)

    drain(pair, p_s)
    drain(agr.at[:, pl.ds(0, NH - 1)], ag_s)
    drain(drecv.at[pl.ds(0, NZ - 1)], d_s)
    drain(fsend.at[:, pl.ds(0, NZ - 1)], f_s)
    drain(gsend.at[:, pl.ds(0, NZ - 1)], g_s)
    drain(srecv.at[pl.ds(0, NH - 1)], s_s)
    if NY > 1:
        drain(yrecv.at[:, pl.ds(0, NY - 1)], y_s)
        drain(zrecv.at[pl.ds(0, NY - 1)], z_s)


def shards(NH, NY, NZ, hidden_in, proj_weight, head_input, gate_input, step_size, decay_rate, norm_gain):
    KD = hidden_in.shape[1]
    SR = STATE // (NZ // 2)
    operands = (hidden_in, proj_weight, head_input, gate_input, step_size.T, decay_rate.reshape(1, HEADS), norm_gain.reshape(1, COLS))
    in_hbm = pl.BlockSpec(memory_space=pltpu.HBM)
    vm, dma = pltpu.VMEM, pltpu.SemaphoreType.DMA
    return pl.pallas_call(
        functools.partial(kernel, NH, NY, NZ),
        name="layer",
        out_shape=jax.ShapeDtypeStruct((T, COLS), BF16),
        in_specs=[in_hbm] * 7,
        out_specs=pl.BlockSpec(memory_space=pltpu.VMEM),
        scratch_shapes=[
            vm((T, KD), BF16), vm((KD, 2 * STATE), BF16), vm((T, COLS), BF16), vm((T, COLS), BF16),
            vm((HEADS, T), F32), vm((1, HEADS), F32), vm((1, COLS), F32), dma((7,)),
            vm((2, 2, T // 2, STATE), F32), vm((2, T // 2, STATE), F32), vm((2, NH, T // 2, STATE), BF16),
            vm((T, COLS), BF16), vm((T, COLS), BF16), vm((T, COLS), F32),
            vm((CHUNKS, NZ, SR, CW), BF16), vm((CHUNKS, NZ, SR, CW), BF16), vm((2, CHUNKS, 1, CW), F32), vm((NZ, CHUNKS, 1, CW), F32),
            vm((CHUNKS, 1, CW), F32), vm((NY, CHUNKS, 1, CW), F32), vm((CHUNKS, SR, CW), F32), vm((CHUNKS, NY, SR, CW), F32),
            vm((CHUNKS, NZ, SR, CW), BF16), vm((CHUNKS, NZ, SR, CW), BF16),
            vm((T, COLS), F32), vm((T, COLS), F32), vm((T, COLS), F32), vm((NH, 1, T), F32),
            dma, dma((2,)), dma, dma((2,)), dma, dma, dma, dma((CHUNKS,)), dma, dma, dma, dma((CHUNKS,)), dma, dma((CHUNKS,)), dma, dma,
            pltpu.SemaphoreType.REGULAR((2,)),
        ],
        compiler_params=pltpu.CompilerParams(collective_id=0, has_side_effects=True, vmem_limit_bytes=20 * 2**20),
    )(*(pltpu.with_memory_space_constraint(operand, pltpu.HBM) for operand in operands))


def solution(mesh):
    NZ = 16
    NY = mesh.shape["seq"] // NZ
    NH = mesh.shape["head"]
    in_specs = (
        P("seq", "head"), P(), P("seq", "head"), P("seq", "head"), P("seq", "head"), P("head"), P("head"),
    )
    return jax.shard_map(
        functools.partial(shards, NH, NY, NZ), mesh=mesh, in_specs=in_specs, out_specs=P("seq", "head"), check_vma=False)
```

```python
import functools
import math

import jax
import jax.numpy as jnp
from jax import lax
from jax.experimental import pallas as pl
from jax.experimental.pallas import tpu as pltpu
from jax.sharding import PartitionSpec as P

MESH = pl.DeviceIdType.MESH
F32, BF16 = jnp.float32, jnp.bfloat16
T = 256
HEADS = 16
HEAD_DIM = 64
STATE = 128
COLS = HEADS * HEAD_DIM
LAG = 1
CHUNKS = 4
CHUNK = COLS // CHUNKS
CW = CHUNK // 2
LOG2E = math.log2(math.e)


def dot(a, b):
    return jnp.dot(a, b, preferred_element_type=F32)


def kernel(
    NH, NY, NZ,
    hid, w, x, g, dt, rate, gain, out,
    hid_v, w_v, x_v, g_v, dt_v, rate_v, gain_v, in_sem,
    part, pair, agr, scl, wgt, expand,
    fsend, frecv, dsend, drecv, zsend, zrecv, ysend, yrecv, gsend, grecv,
    acc, fac, gated_v, srecv,
    p_s, p_r, ag_s, ag_r, d_s, d_r, f_s, f_r, z_s, z_r, y_s, y_r, g_s, g_r, s_s, s_r, token,
):
    KD = hid_v.shape[1]
    NI = NZ // 2
    SR = STATE // NI
    me_h = lax.axis_index("head")
    core = lax.rem(me_h, 2)
    seq = lax.axis_index("seq")
    me_z = lax.rem(seq, NZ)
    me_y = lax.div(seq, NZ)

    def head_peer(r):
        return lax.rem(me_h + r, NH)

    def far_first(k):
        return NZ // 2 + (k // 2 if k % 2 else -(k // 2))

    def z_peer(k):
        return lax.rem(me_z + far_first(k), NZ)

    def y_peer(r):
        return lax.rem(me_y + r, NY)

    def seq_id(y, z):
        return y * NZ + z

    def each_now(n, peer_of, action):
        for r in range(1, n):
            action(peer_of(r))

    def signal(sem, device):
        pl.semaphore_signal(sem, inc=1, device_id=device, device_id_type=MESH)

    loads = [
        pltpu.make_async_copy(hid, hid_v, in_sem.at[0]),
        pltpu.make_async_copy(w.at[pl.ds(pl.multiple_of(me_h * KD, KD), KD)], w_v, in_sem.at[1]),
        pltpu.make_async_copy(dt, dt_v, in_sem.at[2]),
        pltpu.make_async_copy(rate, rate_v, in_sem.at[3]),
        pltpu.make_async_copy(x, x_v, in_sem.at[4]),
        pltpu.make_async_copy(g, g_v, in_sem.at[5]),
        pltpu.make_async_copy(gain, gain_v, in_sem.at[6]),
    ]
    loads[0].start()
    loads[1].start()

    barrier = pltpu.get_barrier_semaphore()
    def greet(sem, distance):
        for step in (distance, NZ - distance):
            signal(sem, {"seq": seq_id(me_y, lax.rem(me_z + step, NZ))})

    for near in range(1, 5):
        greet(barrier, near)
    strides = [4]
    each_now(NY, y_peer, lambda p: signal(barrier, {"seq": seq_id(p, me_z)}))
    each_now(NH, head_peer, lambda p: signal(barrier, {"head": p}))

    for load in loads[2:]:
        load.start()
    loads[0].wait()
    loads[1].wait()
    own = dot(hid_v[...], w_v[...])
    for m in range(2):
        part[m] = own[:, STATE * m:STATE * m + STATE].reshape(2, T // 2, STATE)

    def remote(src, dst, send_sem, recv_sem, device):
        return pltpu.make_async_remote_copy(
            src_ref=src, dst_ref=dst, send_sem=send_sem, recv_sem=recv_sem, device_id=device, device_id_type=MESH)

    def drain(ref, sem):
        pltpu.make_async_copy(ref, ref, sem).wait()

    def pair_copy(m):
        return remote(part.at[m, 1 - core], pair.at[m], p_s, p_r.at[m], {"head": me_h + 1 - 2 * core})

    def ag_copy(m, peer, slot):
        return remote(agr.at[m, slot], agr.at[m, slot], ag_s, ag_r.at[m], {"head": peer})

    def d_copy(peer, slot):
        return remote(dsend.at[lax.div(peer, NI)], drecv.at[slot], d_s, d_r, {"seq": seq_id(me_y, peer)})

    def f_copy(c, peer, slot):
        return remote(fsend.at[c, peer], frecv.at[c, slot], f_s, f_r.at[c], {"seq": seq_id(me_y, peer)})

    def y_copy(c, peer, slot):
        return remote(ysend.at[c], yrecv.at[c, slot], y_s, y_r.at[c], {"seq": seq_id(peer, me_z)})

    def span_copy(peer, slot):
        return remote(zsend, zrecv.at[slot], z_s, z_r, {"seq": seq_id(peer, me_z)})

    def g_copy(c, peer, slot):
        return remote(gsend.at[c, peer], grecv.at[c, slot], g_s, g_r.at[c], {"seq": seq_id(me_y, peer)})

    def s_copy(peer, slot):
        return remote(srecv.at[slot], srecv.at[slot], s_s, s_r, {"head": peer})

    pl.semaphore_wait(barrier, (NH - 1) + (NY - 1) + 8)
    greet(token.at[0], strides[0])
    for m in range(2):
        pair_copy(m).start()

    def spread_chip_sum(m):
        drain(pair.at[m], p_r.at[m])
        agr[m, pl.ds(me_h, 1)] = (part[m, pl.ds(core, 1)] + pair[m][None]).astype(BF16)
        each_now(NH, head_peer, lambda p: ag_copy(m, p, me_h).start())

    spread_chip_sum(0)

    def projected(m):
        drain(agr.at[m, pl.ds(0, NH - 1)], ag_r.at[m])
        halves = []
        for i in range(2):
            total = agr[m, i].astype(F32)
            for k in range(2 + i, NH, 2):
                total = total + agr[m, k].astype(F32)
            halves.append(total)
        return jnp.concatenate(halves, axis=0).astype(BF16)

    loads[2].wait()
    loads[3].wait()
    lane = lax.broadcasted_iota(jnp.int32, (T, 128), 1)
    low_lane = lane < HEAD_DIM
    rows = lax.broadcasted_iota(jnp.int32, (T, T), 0)
    cols = lax.broadcasted_iota(jnp.int32, (T, T), 1)
    causal = rows >= cols
    tri = jnp.where(causal, 1.0, 0.0).astype(BF16)
    dt_all = jnp.concatenate([dt_v[...], jnp.zeros((128 - HEADS, T), F32)], axis=0).T
    rate_all = jnp.concatenate([rate_v[...], jnp.zeros((1, 128 - HEADS), F32)], axis=1)
    log_decay = -(dt_all * rate_all)
    top = log_decay.astype(BF16)
    rest = log_decay - top.astype(F32)
    mid = rest.astype(BF16)
    low = (rest - mid.astype(F32)).astype(BF16)
    cum = ((dot(tri, low) + dot(tri, mid)) + dot(tri, top)) * LOG2E
    cum_end = cum[T - 1:T, :]
    grow = jnp.exp2(cum)
    tail = jnp.exp2(cum_end - cum)

    def spread(value, q):
        a = jnp.broadcast_to(value[:, 2 * q:2 * q + 1], (T, 128))
        b = jnp.broadcast_to(value[:, 2 * q + 1:2 * q + 2], (T, 128))
        return jnp.where(low_lane, a, b)

    for q in range(HEADS // 2):
        at = pl.ds(128 * q, 128)
        e = spread(grow, q)
        expand[:, at] = e
        dsend[q % 2, q // 2] = e[T - 1:T, :]
    for i, stride in enumerate(strides[1:]):
        pl.semaphore_wait(token.at[i], 2)
        greet(token.at[i + 1], stride)

    spread_chip_sum(1)
    loads[4].wait()
    for q in range(HEADS // 2):
        at = pl.ds(128 * q, 128)
        s = (x_v[:, at].astype(F32) * spread(dt_all, q)).astype(BF16)
        scl[:, at] = s
        wgt[:, at] = (spread(tail, q) * s.astype(F32)).astype(BF16)

    pl.semaphore_wait(token.at[len(strides) - 1], 2)
    each_now(NZ, z_peer, lambda p: d_copy(p, me_z).start())
    drecv[pl.ds(me_z, 1)] = dsend[pl.ds(lax.div(me_z, NI), 1)]
    b_cols = projected(0).astype(F32).T.astype(BF16)


    for c in range(CHUNKS):
        fresh = dot(b_cols, wgt[:, pl.ds(CHUNK * c, CHUNK)]).astype(BF16)
        for j in range(2):
            fsend[c, pl.ds(NI * j, NI)] = fresh[:, CW * j:CW * j + CW].reshape(NI, SR, CW)
        each_now(NZ, z_peer, lambda p: f_copy(c, p, me_z).start())
        frecv[c, pl.ds(me_z, 1)] = fsend[c, pl.ds(me_z, 1)]

    c_rows = projected(1)
    loads[5].wait()
    scores = dot(c_rows, b_cols)
    M = T // 2
    tri_half = causal[:M, :M]
    s00 = jnp.where(tri_half, scores[:M, :M], 0.0)
    s10 = scores[M:, :M]
    s11 = jnp.where(tri_half, scores[M:, M:], 0.0)
    cum_rows = cum.T
    for q in range(HEADS // 2):
        at = pl.ds(128 * q, 128)
        mix = []
        for h in (2 * q, 2 * q + 1):
            down = jnp.broadcast_to(cum[:, h:h + 1], (T, M))
            along = cum_rows[h:h + 1, :]
            m00 = s00 * jnp.exp2(jnp.minimum(down[:M] - along[:, :M], 0.0))
            m10 = s10 * jnp.exp2(down[M:] - along[:, :M])
            m11 = s11 * jnp.exp2(jnp.minimum(down[M:] - along[:, M:], 0.0))
            mix.append((m00.astype(BF16), jnp.concatenate([m10.astype(BF16), m11.astype(BF16)], axis=1)))
        s = scl[:, at]
        zero = jnp.zeros_like(s)
        sa = jnp.where(low_lane, s, zero)
        sb = jnp.where(low_lane, zero, s)
        upper = dot(jnp.concatenate([mix[0][0], mix[1][0]], axis=1), jnp.concatenate([sa[:M], sb[:M]], axis=0))
        lower = dot(mix[0][1], sa) + dot(mix[1][1], sb)
        v = g_v[:, at].astype(F32)
        silu = v / (1.0 + jnp.exp(-v))
        fac[:, at] = expand[:, at] * silu
        acc[:M, at] = upper * silu[:M]
        acc[M:, at] = lower * silu[M:]

    drain(drecv.at[pl.ds(0, NZ - 1)], d_r)
    span = drecv[0]
    for k in range(1, NZ):
        span = span * drecv[k]
    zsend[...] = span
    each_now(NY, y_peer, lambda p: span_copy(p, me_y).start())
    zrecv[pl.ds(me_y, 1)] = zsend[...][None]
    def total_of_row(c):
        drain(frecv.at[c, pl.ds(0, NZ - 1)], f_r.at[c])
        carry = frecv[c, 0].astype(F32)
        for k in range(1, NZ):
            carry = drecv[k, c] * carry + frecv[c, k].astype(F32)
        ysend[c] = carry
        each_now(NY, y_peer, lambda p: y_copy(c, p, me_y).start())
        yrecv[c, pl.ds(me_y, 1)] = ysend[c][None]

    def entering_states(c):
        if NY > 1:
            drain(yrecv.at[c, pl.ds(0, NY - 1)], y_r.at[c])
        carry = jnp.zeros((SR, CW), F32)
        for k in range(NY - 1):
            later = zrecv[k, c] * carry + yrecv[c, k]
            carry = jnp.where(k < me_y, later, carry)
        for k in range(NZ):
            gsend[c, k] = carry.astype(BF16)
            carry = drecv[k, c] * carry + frecv[c, k].astype(F32)
        each_now(NZ, z_peer, lambda p: g_copy(c, p, me_z).start())
        grecv[c, pl.ds(me_z, 1)] = gsend[c, pl.ds(me_z, 1)]

    for c in range(CHUNKS + LAG):
        if c < CHUNKS:
            total_of_row(c)
        if c == 0 and NY > 1:
            drain(zrecv.at[pl.ds(0, NY - 1)], z_r)
        if c >= LAG:
            entering_states(c - LAG)

    loads[6].wait()
    squares = jnp.zeros((T, 128), F32)
    for c in range(CHUNKS):
        drain(grecv.at[c, pl.ds(0, NZ - 1)], g_r.at[c])
        for j in range(2):
            entering = grecv[c, pl.ds(NI * j, NI)].reshape(STATE, CW)
            at = pl.ds(CHUNK * c + CW * j, CW)
            gated = acc[:, at] + dot(c_rows, entering) * fac[:, at]
            gated_v[:, at] = gated * gain_v[:, at]
            sq = gated * gated
            for i in range(CW // 128):
                squares = squares + sq[:, 128 * i:128 * i + 128]
    srecv[pl.ds(me_h, 1)] = jnp.sum(squares.T, axis=0, keepdims=True)[None]
    each_now(NH, head_peer, lambda p: s_copy(p, me_h).start())
    drain(srecv.at[pl.ds(0, NH - 1)], s_r)
    mean = srecv[0]
    for k in range(1, NH):
        mean = mean + srecv[k]
    mean = mean / (NH * COLS)
    scale = lax.rsqrt(jnp.broadcast_to(mean, (128, T)) + 1e-05).T
    for q in range(HEADS // 2):
        at = pl.ds(128 * q, 128)
        out[:, at] = (gated_v[:, at] * scale).astype(BF16)

    drain(pair, p_s)
    drain(agr.at[:, pl.ds(0, NH - 1)], ag_s)
    drain(drecv.at[pl.ds(0, NZ - 1)], d_s)
    drain(fsend.at[:, pl.ds(0, NZ - 1)], f_s)
    drain(gsend.at[:, pl.ds(0, NZ - 1)], g_s)
    drain(srecv.at[pl.ds(0, NH - 1)], s_s)
    if NY > 1:
        drain(yrecv.at[:, pl.ds(0, NY - 1)], y_s)
        drain(zrecv.at[pl.ds(0, NY - 1)], z_s)


def shards(NH, NY, NZ, hidden_in, proj_weight, head_input, gate_input, step_size, decay_rate, norm_gain):
    KD = hidden_in.shape[1]
    SR = STATE // (NZ // 2)
    operands = (hidden_in, proj_weight, head_input, gate_input, step_size.T, decay_rate.reshape(1, HEADS), norm_gain.reshape(1, COLS))
    in_hbm = pl.BlockSpec(memory_space=pltpu.HBM)
    vm, dma = pltpu.VMEM, pltpu.SemaphoreType.DMA
    return pl.pallas_call(
        functools.partial(kernel, NH, NY, NZ),
        name="layer",
        out_shape=jax.ShapeDtypeStruct((T, COLS), BF16),
        in_specs=[in_hbm] * 7,
        out_specs=pl.BlockSpec(memory_space=pltpu.VMEM),
        scratch_shapes=[
            vm((T, KD), BF16), vm((KD, 2 * STATE), BF16), vm((T, COLS), BF16), vm((T, COLS), BF16),
            vm((HEADS, T), F32), vm((1, HEADS), F32), vm((1, COLS), F32), dma((7,)),
            vm((2, 2, T // 2, STATE), F32), vm((2, T // 2, STATE), F32), vm((2, NH, T // 2, STATE), BF16),
            vm((T, COLS), BF16), vm((T, COLS), BF16), vm((T, COLS), F32),
            vm((CHUNKS, NZ, SR, CW), BF16), vm((CHUNKS, NZ, SR, CW), BF16), vm((2, CHUNKS, 1, CW), F32), vm((NZ, CHUNKS, 1, CW), F32),
            vm((CHUNKS, 1, CW), F32), vm((NY, CHUNKS, 1, CW), F32), vm((CHUNKS, SR, CW), F32), vm((CHUNKS, NY, SR, CW), F32),
            vm((CHUNKS, NZ, SR, CW), BF16), vm((CHUNKS, NZ, SR, CW), BF16),
            vm((T, COLS), F32), vm((T, COLS), F32), vm((T, COLS), F32), vm((NH, 1, T), F32),
            dma, dma((2,)), dma, dma((2,)), dma, dma, dma, dma((CHUNKS,)), dma, dma, dma, dma((CHUNKS,)), dma, dma((CHUNKS,)), dma, dma,
            pltpu.SemaphoreType.REGULAR((2,)),
        ],
        compiler_params=pltpu.CompilerParams(collective_id=0, has_side_effects=True, vmem_limit_bytes=20 * 2**20),
    )(*(pltpu.with_memory_space_constraint(operand, pltpu.HBM) for operand in operands))


def solution(mesh):
    NZ = 16
    NY = mesh.shape["seq"] // NZ
    NH = mesh.shape["head"]
    in_specs = (
        P("seq", "head"), P(), P("seq", "head"), P("seq", "head"), P("seq", "head"), P("head"), P("head"),
    )
    return jax.shard_map(
        functools.partial(shards, NH, NY, NZ), mesh=mesh, in_specs=in_specs, out_specs=P("seq", "head"), check_vma=False)
```
